32 devices in a mesh: dp: 8 (over z, core), tensor: 4 (over y, x).
Axes of the slice: x: 2, y: 2, z: 4, core: 2. Of those that a mesh axis runs over, the one named last changes fastest.
Arguments:
- tokens: bfloat16 [65536, 1024], P(('dp', 'tensor')), may hold values from -6 to 6
- cotangent: bfloat16 [65536, 1024], P(('dp', 'tensor')), may hold values from -6 to 6
- clip_counts: int32 [8], P('dp'), may hold values from 1 to 8, as said below
- norm_params: float32 [6, 1024], replicated, as said below
- head_bias: float32 [2, 1024], replicated, may hold values from -1.75 to 1.75
- up_bias: float32 [4096], replicated, may hold values from -1.75 to 1.75
- w_qkv: float32 [1024, 3, 1024], P(None, None, 'tensor'), may hold values from -0.1875 to 0.1875
- w_out: float32 [1024, 1024], P('tensor'), may hold values from -0.75 to 0.75
- w_up: float32 [1024, 4096], P(None, 'tensor'), may hold values from -0.1875 to 0.1875
- w_down: float32 [4096, 1024], P('tensor'), may hold values from -0.125 to 0.125
- mom_norm: float32 [6, 1024], replicated, may hold values from -128 to 128
- mom_head_bias: float32 [2, 1024], replicated, may hold values from -128 to 128
- mom_up_bias: float32 [4096], replicated, may hold values from -128 to 128
- mom_qkv: float32 [1024, 3, 1024], P(None, None, 'tensor'), may hold values from -128 to 128
- mom_out: float32 [1024, 1024], P('tensor'), may hold values from -128 to 128
- mom_up: float32 [1024, 4096], P(None, 'tensor'), may hold values from -128 to 128
- mom_down: float32 [4096, 1024], P('tensor'), may hold values from -128 to 128
- err_qkv: float32 [8, 1024, 3, 1024], P('dp', None, None, 'tensor'), may hold values from -128 to 128
- err_out: float32 [8, 1024, 1024], P('dp', 'tensor'), may hold values from -128 to 128
- err_up: float32 [8, 1024, 4096], P('dp', None, 'tensor'), may hold values from -128 to 128
- err_down: float32 [8, 4096, 1024], P('dp', 'tensor'), may hold values from -128 to 128
- basis_qkv: float32 [4, 768, 8], P('tensor'), may hold values from -6 to 6
- basis_out: float32 [4, 1024, 8], P('tensor'), may hold values from -6 to 6
- basis_up: float32 [4, 1024, 8], P('tensor'), may hold values from -6 to 6
- basis_down: float32 [4, 1024, 8], P('tensor'), may hold values from -6 to 6
Outputs:
- block_out: bfloat16 [65536, 1024], P(('dp', 'tensor'))
- input_grad: bfloat16 [65536, 1024], P(('dp', 'tensor'))
- new_norm_params: float32 [6, 1024], replicated
- new_head_bias: float32 [2, 1024], replicated
- new_up_bias: float32 [4096], replicated
- new_w_qkv: float32 [1024, 3, 1024], P(None, None, 'tensor')
- new_w_out: float32 [1024, 1024], P('tensor')
- new_w_up: float32 [1024, 4096], P(None, 'tensor')
- new_w_down: float32 [4096, 1024], P('tensor')
- new_mom_norm: float32 [6, 1024], replicated
- new_mom_head_bias: float32 [2, 1024], replicated
- new_mom_up_bias: float32 [4096], replicated
- new_mom_qkv: float32 [1024, 3, 1024], P(None, None, 'tensor')
- new_mom_out: float32 [1024, 1024], P('tensor')
- new_mom_up: float32 [1024, 4096], P(None, 'tensor')
- new_mom_down: float32 [4096, 1024], P('tensor')
- new_err_qkv: float32 [8, 1024, 3, 1024], P('dp', None, None, 'tensor')
- new_err_out: float32 [8, 1024, 1024], P('dp', 'tensor')
- new_err_up: float32 [8, 1024, 4096], P('dp', None, 'tensor')
- new_err_down: float32 [8, 4096, 1024], P('dp', 'tensor')
- new_p_qkv: float32 [4, 1024, 8], P('tensor')
- new_p_out: float32 [4, 256, 8], P('tensor')
- new_p_up: float32 [4, 1024, 8], P('tensor')
- new_p_down: float32 [4, 1024, 8], P('tensor')
- new_q_qkv: float32 [4, 768, 8], P('tensor')
- new_q_out: float32 [4, 1024, 8], P('tensor')
- new_q_up: float32 [4, 1024, 8], P('tensor')
- new_q_down: float32 [4, 1024, 8], P('tensor')
The draws below stay inside these ranges and needn't reach their ends.
Inputs may be any that keep to these rules, and one draw needn't show every extreme that they name: `clip_counts`: the number of live clips of each data replica; in every draw some replica holds 8 live clips and some other holds 1. `norm_params`: rows 0 and 3 are gains near 1; rows 1, 2, 4 and 5 are shifts and biases.
All inputs are finite; a program needn't handle non-finite values.
Results may differ from the reference program's by a relative error of at most 0.03.
Values may be sent and summed in bfloat16 or wider, within the bound.
No kernel may reach another device: no remote copies, remote signals or barrier semaphores. Data moves between devices by JAX's collectives and lax.ppermute only.
A program may use at most 384 MiB of HBM per device.

```python
import jax
import jax.numpy as jnp
from jax import lax

D = 1024
HEADS = 16
HEAD_DIM = 64
FF = 4096
RANK = 8
CLIP_LEN = 1024
CLIPS = 8
TOKENS = 65536
N_DP = 8
N_TENSOR = 4


def draw_clip_counts(key, part):
    counts = jax.random.randint(jax.random.fold_in(key, 11), (N_DP,), 1, CLIPS + 1)
    fullest = jax.random.randint(jax.random.fold_in(key, 12), (), 0, N_DP)
    emptiest = (fullest + 1 + jax.random.randint(jax.random.fold_in(key, 13), (), 0, N_DP - 1)) % N_DP
    positions = jnp.arange(N_DP)
    counts = jnp.where(positions == fullest, CLIPS, counts)
    counts = jnp.where(positions == emptiest, 1, counts)
    return counts.astype(jnp.int32)


def draw_norm_params(key, part):
    centres = jnp.array([1.0, 0.0, 0.0, 1.0, 0.0, 0.0], jnp.float32)[:, None]
    spreads = jnp.array([0.2, 0.3, 0.3, 0.2, 0.3, 0.3], jnp.float32)[:, None]
    noise = jax.random.normal(jax.random.fold_in(key, 21), (6, D), jnp.float32)
    return centres + spreads * noise


def levels(stream_key, extent, split, smallest, largest):
    factor_of, own = 1.0, jax.random.fold_in(stream_key, 6)
    for position, blocks in split:
        steps = jnp.exp(jax.random.uniform(jax.random.fold_in(own, position), (blocks,), jnp.float32, smallest / len(split), largest / len(split)))
        factor_of = factor_of * jnp.repeat(steps, extent[position] // blocks).reshape([-1 if axis == position else 1 for axis in range(len(extent))])
    return factor_of


def bell_draw(key, dims, deviation, reach, pieces=(), held_as=jnp.bfloat16):
    factor_of = levels(key, dims, pieces, -0.22, 0.18) if pieces else 1.0
    values = jax.random.normal(key, dims, jnp.float32) * deviation * factor_of
    return jnp.minimum(jnp.maximum(values, -reach), reach).astype(held_as)


def setup_inputs(seed: int = 0) -> dict:
    key_of = jax.random.split(jax.random.key(seed), 26)
    return {
        "tokens": bell_draw(key_of[0], (TOKENS, D), 1.0, 6.0, ((0, 32),)),
        "cotangent": bell_draw(key_of[1], (TOKENS, D), 1.0, 6.0, ((0, 32),)),
        "clip_counts": draw_clip_counts(jax.random.fold_in(key_of[25], 71), 0),
        "norm_params": draw_norm_params(jax.random.fold_in(key_of[25], 71), 0),
        "head_bias": bell_draw(key_of[4], (2, D), 0.3, 1.75, (), jnp.float32),
        "up_bias": bell_draw(key_of[5], (FF,), 0.3, 1.75, (), jnp.float32),
        "w_qkv": bell_draw(key_of[6], (D, 3, D), D ** -0.5, 0.1875, ((2, 4),), jnp.float32),
        "w_out": bell_draw(key_of[7], (D, D), (D // 16) ** -0.5, 0.75, ((0, 4),), jnp.float32),
        "w_up": bell_draw(key_of[8], (D, FF), D ** -0.5, 0.1875, ((1, 4),), jnp.float32),
        "w_down": bell_draw(key_of[9], (FF, D), (FF // 2) ** -0.5, 0.125, ((0, 4),), jnp.float32),
        "mom_norm": bell_draw(key_of[10], (6, D), 20.0, 128.0, (), jnp.float32),
        "mom_head_bias": bell_draw(key_of[11], (2, D), 20.0, 128.0, (), jnp.float32),
        "mom_up_bias": bell_draw(key_of[12], (FF,), 20.0, 128.0, (), jnp.float32),
        "mom_qkv": bell_draw(key_of[13], (D, 3, D), 20.0, 128.0, ((2, 4),), jnp.float32),
        "mom_out": bell_draw(key_of[14], (D, D), 20.0, 128.0, ((0, 4),), jnp.float32),
        "mom_up": bell_draw(key_of[15], (D, FF), 20.0, 128.0, ((1, 4),), jnp.float32),
        "mom_down": bell_draw(key_of[16], (FF, D), 20.0, 128.0, ((0, 4),), jnp.float32),
        "err_qkv": bell_draw(key_of[17], (N_DP, D, 3, D), 20.0, 128.0, ((0, 8), (3, 4)), jnp.float32),
        "err_out": bell_draw(key_of[18], (N_DP, D, D), 20.0, 128.0, ((0, 8), (1, 4)), jnp.float32),
        "err_up": bell_draw(key_of[19], (N_DP, D, FF), 20.0, 128.0, ((0, 8), (2, 4)), jnp.float32),
        "err_down": bell_draw(key_of[20], (N_DP, FF, D), 20.0, 128.0, ((0, 8), (1, 4)), jnp.float32),
        "basis_qkv": bell_draw(key_of[21], (N_TENSOR, 3 * D // N_TENSOR, RANK), 1.0, 6.0, ((0, 4),), jnp.float32),
        "basis_out": bell_draw(key_of[22], (N_TENSOR, D, RANK), 1.0, 6.0, ((0, 4),), jnp.float32),
        "basis_up": bell_draw(key_of[23], (N_TENSOR, FF // N_TENSOR, RANK), 1.0, 6.0, ((0, 4),), jnp.float32),
        "basis_down": bell_draw(key_of[24], (N_TENSOR, D, RANK), 1.0, 6.0, ((0, 4),), jnp.float32),
    }


PRECISE = lax.Precision.HIGHEST
NORM_EPS = 1e-06
STEP_RATE = 0.001
VECTOR_RATE = 0.015
MOMENTUM_DECAY = 0.9

@jax.custom_vjp
def low(v):
    return lax.optimization_barrier(v.astype(jnp.bfloat16)).astype(jnp.float32)

@jax.custom_vjp
def low_back(v):
    return v

def low_keep(v):
    return (low(v), None)

def low_pass(kept, grad):
    return (grad,)

def back_keep(v):
    return (v, None)

def back_low(kept, grad):
    return (low(grad),)
low.defvjp(low_keep, low_pass)
low_back.defvjp(back_keep, back_low)

def layer_norm(values):
    centre = values - lax.optimization_barrier(jnp.mean(values, axis=-1, keepdims=True))
    spread = lax.optimization_barrier(jnp.mean(centre * centre, axis=-1, keepdims=True))
    return centre * lax.rsqrt(spread + NORM_EPS)

def orthonormal(factor):
    columns = []
    for column_pos in range(factor.shape[-1]):
        vector = factor[..., column_pos]
        for column in columns:
            vector = vector - lax.optimization_barrier(jnp.sum(column * vector, axis=-1, keepdims=True)) * column
        vector = vector * lax.rsqrt(lax.optimization_barrier(jnp.sum(vector * vector, axis=-1, keepdims=True)) + 1e-12)
        columns.append(vector)
    return jnp.stack(columns, axis=-1)

def attend_clip(operands):
    queries, key_vecs, val_vecs = operands
    scale_qk = queries.shape[-1] ** (-0.5)
    scores = low_back(jnp.einsum('qhd,khd->hqk', queries, key_vecs, precision=PRECISE) * scale_qk)
    attn_prob = jax.nn.softmax(scores, axis=-1)
    return jnp.einsum('hqk,khd->qhd', low(attn_prob), val_vecs, precision=PRECISE)

def forward(params, inputs):
    norm_params, head_bias, up_bias, w_qkv, w_out, w_up, w_down = params
    row_count = inputs.shape[0]
    ln_one = low(layer_norm(inputs) * norm_params[0] + norm_params[1])
    bias_qkv = jnp.stack([head_bias[0], jnp.zeros_like(head_bias[0]), head_bias[1]])
    qkv_rows = jnp.einsum('td,dcf->tcf', ln_one, low(w_qkv), precision=PRECISE) + bias_qkv
    qkv_rows = low(low_back(qkv_rows)).reshape(CLIPS, CLIP_LEN, 3, HEADS, HEAD_DIM)
    context = lax.map(jax.checkpoint(attend_clip), (qkv_rows[:, :, 0], qkv_rows[:, :, 1], qkv_rows[:, :, 2]))
    context = low(low_back(context)).reshape(row_count, D)
    attn_sum = low_back(jnp.dot(context, low(w_out), precision=PRECISE))
    resid_one = inputs + attn_sum + norm_params[2]
    ln_two = low(layer_norm(resid_one) * norm_params[3] + norm_params[4])
    pre_act = low_back(jnp.dot(ln_two, low(w_up), precision=PRECISE) + up_bias)
    hidden = low(jax.nn.gelu(pre_act, approximate=False))
    ffn_sum = low_back(jnp.dot(hidden, low(w_down), precision=PRECISE))
    return resid_one + ffn_sum + norm_params[5]

def view_qkv(whole_mat):
    leading = whole_mat.shape[:-3]
    width_loc = D // N_TENSOR
    split_up = whole_mat.reshape(leading + (D, 3, N_TENSOR, width_loc))
    return jnp.moveaxis(split_up, -2, -4).reshape(leading + (N_TENSOR, D, 3 * width_loc))

def unview_qkv(view_mat):
    leading = view_mat.shape[:-3]
    width_loc = D // N_TENSOR
    split_up = view_mat.reshape(leading + (N_TENSOR, D, 3, width_loc))
    return jnp.moveaxis(split_up, -4, -2).reshape(leading + (D, 3, D))

def view_rows(whole_mat):
    leading = whole_mat.shape[:-2]
    return whole_mat.reshape(leading + (N_TENSOR, whole_mat.shape[-2] // N_TENSOR, whole_mat.shape[-1]))

def unview_rows(view_mat):
    leading = view_mat.shape[:-3]
    return view_mat.reshape(leading + (view_mat.shape[-3] * view_mat.shape[-2], view_mat.shape[-1]))

def view_cols(whole_mat):
    leading = whole_mat.shape[:-2]
    split_up = whole_mat.reshape(leading + (whole_mat.shape[-2], N_TENSOR, whole_mat.shape[-1] // N_TENSOR))
    return jnp.moveaxis(split_up, -2, -3)

def unview_cols(view_mat):
    leading = view_mat.shape[:-3]
    moved_axes = jnp.moveaxis(view_mat, -3, -2)
    return moved_axes.reshape(leading + (view_mat.shape[-2], view_mat.shape[-3] * view_mat.shape[-1]))

def compress(grad_view, err_view, factor):
    merged = grad_view + err_view
    left_sum = jnp.einsum('rtmn,tnk->tmk', merged, factor, precision=PRECISE)
    ortho_left = orthonormal(left_sum)
    right_mean = jnp.einsum('rtmn,tmk->tnk', merged, ortho_left, precision=PRECISE) / N_DP
    approx = jnp.einsum('tmk,tnk->tmn', ortho_left, right_mean, precision=PRECISE)
    return (approx, merged - approx[None], ortho_left, right_mean)

def reference(tokens, cotangent, clip_counts, norm_params, head_bias, up_bias, w_qkv, w_out, w_up, w_down, mom_norm, mom_head_bias, mom_up_bias, mom_qkv, mom_out, mom_up, mom_down, err_qkv, err_out, err_up, err_down, basis_qkv, basis_out, basis_up, basis_down):
    rep_rows = CLIPS * CLIP_LEN
    inputs_all = tokens.astype(jnp.float32).reshape(N_DP, rep_rows, D)
    clip_of_row = jnp.arange(rep_rows, dtype=jnp.int32) // CLIP_LEN
    live_rows = (clip_of_row[None, :] < clip_counts[:, None]).astype(jnp.float32)
    grads_all = cotangent.astype(jnp.float32).reshape(N_DP, rep_rows, D) * live_rows[:, :, None]
    params = (norm_params, head_bias, up_bias, w_qkv, w_out, w_up, w_down)

    def replica(operands):
        inputs, grad_out = operands
        output, pull_back = jax.vjp(forward, params, inputs)
        grad_params, grad_in = pull_back(grad_out)
        return (output, grad_in, grad_params)
    outputs, grad_inputs, grad_params = lax.map(replica, (inputs_all, grads_all))
    block_out = outputs.reshape(TOKENS, D).astype(jnp.bfloat16)
    input_grad = grad_inputs.reshape(TOKENS, D).astype(jnp.bfloat16)
    new_vecs = []
    new_vec_moms = []
    for param_now, moment_now, grad_now in zip((norm_params, head_bias, up_bias), (mom_norm, mom_head_bias, mom_up_bias), grad_params[:3]):
        moment_new = MOMENTUM_DECAY * moment_now + lax.optimization_barrier(jnp.sum(grad_now, axis=0)) / N_DP
        new_vec_moms.append(moment_new)
        new_vecs.append(param_now - VECTOR_RATE * moment_new)
    weights = (w_qkv, w_out, w_up, w_down)
    moments = (mom_qkv, mom_out, mom_up, mom_down)
    errors = (err_qkv, err_out, err_up, err_down)
    factors = (basis_qkv, basis_out, basis_up, basis_down)
    views = ((view_qkv, unview_qkv), (view_rows, unview_rows), (view_cols, unview_cols), (view_rows, unview_rows))
    new_weights = []
    new_moments = []
    new_errors = []
    new_lefts = []
    new_rights = []
    for weight, moment, error, factor, grad_now, view_pair in zip(weights, moments, errors, factors, grad_params[3:], views):
        to_view, from_view = view_pair
        approx, err_view, ortho_left, right_mean = compress(to_view(grad_now), to_view(error), factor)
        moment_new = MOMENTUM_DECAY * moment + from_view(approx)
        new_moments.append(moment_new)
        new_weights.append(weight - STEP_RATE * moment_new)
        new_errors.append(from_view(err_view))
        new_lefts.append(ortho_left)
        new_rights.append(right_mean)
    return (block_out, input_grad, new_vecs[0], new_vecs[1], new_vecs[2], new_weights[0], new_weights[1], new_weights[2], new_weights[3], new_vec_moms[0], new_vec_moms[1], new_vec_moms[2], new_moments[0], new_moments[1], new_moments[2], new_moments[3], new_errors[0], new_errors[1], new_errors[2], new_errors[3], new_lefts[0], new_lefts[1], new_lefts[2], new_lefts[3], new_rights[0], new_rights[1], new_rights[2], new_rights[3])
```

```python
import functools

import jax
import jax.numpy as jnp
from jax import lax
from jax.experimental import pallas as pl
from jax.experimental.pallas import tpu as pltpu
from jax.sharding import PartitionSpec as P

HEAD_DIM = 64
CLIP_LEN = 1024
LANES = 128

PRECISE = lax.Precision.HIGHEST
NORM_EPS = 1e-06
STEP_RATE = 0.001
VECTOR_RATE = 0.015
MOMENTUM_DECAY = 0.9


def layer_norm(values):
    centre = values - jnp.mean(values, axis=-1, keepdims=True)
    spread = jnp.mean(centre * centre, axis=-1, keepdims=True)
    inv_std = lax.rsqrt(spread + NORM_EPS)
    return (centre * inv_std, inv_std)


def norm_back(grad_norm, normed, inv_std):
    mean_grad = jnp.mean(grad_norm, axis=-1, keepdims=True)
    mean_cross = jnp.mean(grad_norm * normed, axis=-1, keepdims=True)
    return inv_std * (grad_norm - mean_grad - normed * mean_cross)


def dot_on(left_dim, right_dim, left_mat, right_mat, precision=None):
    return lax.dot_general(
        left_mat,
        right_mat,
        (((left_dim,), (right_dim,)), ((), ())),
        precision=precision,
        preferred_element_type=jnp.float32,
    )


inner_rows = functools.partial(dot_on, 0, 0)
times_trans = functools.partial(dot_on, 1, 1)
times = functools.partial(dot_on, 1, 0)


def gelu_parts(pre_act):
    size = jnp.abs(pre_act) * (0.5**0.5)
    bell = jnp.exp(-size * size)
    inv = 1.0 / (1.0 + 0.3275911 * size)
    series = 1.061405429 * inv - 1.453152027
    series = series * inv + 1.421413741
    series = series * inv - 0.284496736
    series = series * inv + 0.254829592
    tail = 0.5 * series * inv * bell
    cdf = jnp.where(pre_act >= 0, 1.0 - tail, tail)
    return (pre_act * cdf, cdf + pre_act * bell * 0.3989422804014327)


def head_masks(rows):
    lane = lax.broadcasted_iota(jnp.int32, (rows, LANES), 1)
    return [lane // HEAD_DIM == pos for pos in range(LANES // HEAD_DIM)]


def only(mask, values):
    return jnp.where(mask, values, jnp.zeros_like(values))


def forward_body(scale, tile, q_ref, k_ref, v_ref, ctx_ref, lse_ref, k_heads, v_heads):
    masks = head_masks(k_ref.shape[0])
    for pos, mask in enumerate(masks):
        k_heads[pos] = only(mask, k_ref[...])
        v_heads[pos, :, :LANES] = only(mask, v_ref[...])
        v_heads[pos, :, LANES:] = mask.astype(jnp.bfloat16)
    tile_masks = head_masks(tile)

    def step(pos, carry):
        rows = pl.ds(pl.multiple_of(pos * tile, tile), tile)
        q_tile = q_ref[rows, :] * scale
        total = jnp.zeros((tile, 2 * LANES), jnp.float32)
        tops = []
        for head in range(len(masks)):
            scores = times_trans(q_tile, k_heads[head])
            top = jnp.max(scores, axis=1, keepdims=True)
            weights = jnp.exp(scores - top).astype(jnp.bfloat16)
            total = total + times(weights, v_heads[head])
            tops.append(top)
        sums = total[:, LANES:]
        ctx_ref[rows, :] = (total[:, :LANES] / sums).astype(jnp.bfloat16)
        lse_ref[rows, :] = jnp.where(tile_masks[0], tops[0], tops[1]) + jnp.log(sums)
        return carry

    lax.fori_loop(0, q_ref.shape[0] // tile, step, 0, unroll=True)


def backward_body(
    scale, tile, q_ref, k_ref, v_ref, ctx_ref, lse_ref, do_ref, dq_ref, dk_ref, dv_ref, k_heads, v_heads, dk_sum, dv_sum
):
    masks = head_masks(k_ref.shape[0])
    for pos, mask in enumerate(masks):
        k_heads[pos] = only(mask, k_ref[...])
        v_heads[pos] = only(mask, v_ref[...])
    tile_masks = head_masks(tile)
    dk_sum[...] = jnp.zeros_like(dk_sum)
    dv_sum[...] = jnp.zeros_like(dv_sum)

    def step(pos, carry):
        rows = pl.ds(pl.multiple_of(pos * tile, tile), tile)
        q_tile = q_ref[rows, :] * scale
        do_tile = do_ref[rows, :]
        lse = lse_ref[rows, :]
        cross = do_tile.astype(jnp.float32) * ctx_ref[rows, :].astype(jnp.float32)
        grad_q = jnp.zeros((tile, LANES), jnp.float32)
        for head, mask in enumerate(tile_masks):
            scores = times_trans(q_tile, k_heads[head])
            lane = head * HEAD_DIM
            probs = jnp.exp(scores - lse[:, lane : lane + 1])
            inner = jnp.sum(only(mask, cross), axis=1, keepdims=True)
            grad_p = times_trans(do_tile, v_heads[head])
            grad_s = (probs * (grad_p - inner)).astype(jnp.bfloat16)
            grad_q = grad_q + times(grad_s, k_heads[head])
            dk_sum[...] += inner_rows(grad_s, only(mask, q_tile))
            dv_sum[...] += inner_rows(probs.astype(jnp.bfloat16), only(mask, do_tile))
        dq_ref[rows, :] = (grad_q * scale).astype(jnp.bfloat16)
        return carry

    lax.fori_loop(0, q_ref.shape[0] // tile, step, 0, unroll=True)
    dk_ref[...] = dk_sum[...].astype(jnp.bfloat16)
    dv_ref[...] = dv_sum[...].astype(jnp.bfloat16)


def joined_forward(scale, tile, qkv_ref, *refs):
    parts = [qkv_ref.at[:, pos * LANES : (pos + 1) * LANES] for pos in range(3)]
    forward_body(scale, tile, *parts, *refs)


def joined_backward(scale, tile, qkv_ref, ctx_ref, lse_ref, do_ref, grad_ref, *scratch):
    parts = [qkv_ref.at[:, pos * LANES : (pos + 1) * LANES] for pos in range(3)]
    grads = [grad_ref.at[:, pos * LANES : (pos + 1) * LANES] for pos in range(3)]
    backward_body(scale, tile, *parts, ctx_ref, lse_ref, do_ref, *grads, *scratch)


def block_of(rows, width):
    return pl.BlockSpec((rows, width), lambda clip, block: (clip, block))


def attention_forward(arrays, clips, tile=256):
    joined = len(arrays) == 1
    q_rows, k_rows = arrays[0].shape[0] // clips, arrays[-1].shape[0] // clips
    blocks = arrays[0].shape[1] // (LANES * (3 if joined else 1))
    work = clips * blocks * 2 * q_rows * k_rows
    in_specs = [block_of(q_rows, 3 * LANES)] if joined else [block_of(q_rows, LANES), block_of(k_rows, LANES), block_of(k_rows, LANES)]
    return pl.pallas_call(
        functools.partial(joined_forward if joined else forward_body, HEAD_DIM**-0.5, min(tile, q_rows)),
        grid=(clips, blocks),
        in_specs=in_specs,
        out_specs=[block_of(q_rows, LANES), block_of(q_rows, LANES)],
        out_shape=[
            jax.ShapeDtypeStruct((clips * q_rows, blocks * LANES), dtype)
            for dtype in (jnp.bfloat16, jnp.float32)
        ],
        scratch_shapes=[
            pltpu.VMEM((2, k_rows, LANES), jnp.bfloat16),
            pltpu.VMEM((2, k_rows, 2 * LANES), jnp.bfloat16),
        ],
        cost_estimate=pl.CostEstimate(
            flops=1024 * work, transcendentals=work, bytes_accessed=12 * clips * blocks * q_rows * LANES
        ),
        name="attn_fwd",
    )(*arrays)


def attention_backward(arrays, ctx, lse, grad_ctx, clips, tile=256):
    joined = len(arrays) == 1
    q_rows, k_rows = arrays[0].shape[0] // clips, arrays[-1].shape[0] // clips
    blocks = ctx.shape[1] // LANES
    work = clips * blocks * 2 * q_rows * k_rows
    shared = [block_of(q_rows, LANES) for _ in range(3)]
    if joined:
        in_specs = [block_of(q_rows, 3 * LANES)] + shared
        out_specs = [block_of(q_rows, 3 * LANES)]
        out_shape = [jax.ShapeDtypeStruct(arrays[0].shape, jnp.bfloat16)]
    else:
        in_specs = [block_of(q_rows, LANES), block_of(k_rows, LANES), block_of(k_rows, LANES)] + shared
        out_specs = [block_of(q_rows, LANES), block_of(k_rows, LANES), block_of(k_rows, LANES)]
        out_shape = [jax.ShapeDtypeStruct(array.shape, jnp.bfloat16) for array in arrays]
    return pl.pallas_call(
        functools.partial(joined_backward if joined else backward_body, HEAD_DIM**-0.5, min(tile, q_rows)),
        grid=(clips, blocks),
        in_specs=in_specs,
        out_specs=out_specs,
        out_shape=out_shape,
        scratch_shapes=[
            pltpu.VMEM((2, k_rows, LANES), jnp.bfloat16),
            pltpu.VMEM((2, k_rows, LANES), jnp.bfloat16),
            pltpu.VMEM((k_rows, LANES), jnp.float32),
            pltpu.VMEM((k_rows, LANES), jnp.float32),
        ],
        cost_estimate=pl.CostEstimate(
            flops=2560 * work, transcendentals=work, bytes_accessed=20 * clips * blocks * q_rows * LANES
        ),
        name="attn_bwd",
    )(*arrays, ctx, lse, grad_ctx)


def orthonormal_body(count, *refs):
    values = [ref[...] for ref in refs[:count]]
    rank = values[0].shape[0]
    rows = [lax.broadcasted_iota(jnp.int32, (rank, 1), 0) for _ in values]
    for pos in range(rank):
        for which, value in enumerate(values):
            vector = value[pos : pos + 1, :]
            vector = vector * lax.rsqrt(jnp.sum(vector * vector, axis=1, keepdims=True) + 1e-12)
            along = jnp.sum(value * vector, axis=1, keepdims=True)
            later = jnp.where(rows[which] > pos, value - along * vector, value)
            values[which] = jnp.where(rows[which] == pos, vector, later)
    for ref, value in zip(refs[count:], values):
        ref[...] = value


def orthonormal(lefts):
    return pl.pallas_call(
        functools.partial(orthonormal_body, len(lefts)),
        out_shape=[jax.ShapeDtypeStruct(left.shape, jnp.float32) for left in lefts],
        name="orthonormal",
    )(*lefts)


def psum_joined(parts, axis):
    joined = lax.psum(jnp.concatenate(parts, axis=1).astype(jnp.bfloat16), axis).astype(jnp.float32)
    ends = [0]
    for part in parts:
        ends.append(ends[-1] + part.shape[1])
    return [joined[:, start:end] for start, end in zip(ends, ends[1:])]


def shards(
    tokens,
    cotangent,
    clip_counts,
    norm_params,
    head_bias,
    up_bias,
    w_qkv,
    w_out,
    w_up,
    w_down,
    mom_norm,
    mom_head_bias,
    mom_up_bias,
    mom_qkv,
    mom_out,
    mom_up,
    mom_down,
    err_qkv,
    err_out,
    err_up,
    err_down,
    basis_qkv,
    basis_out,
    basis_up,
    basis_down,
):
    tensor_count = lax.axis_size("tensor")
    tensor_pos = lax.axis_index("tensor")
    replica_count = lax.axis_size("dp")
    local_rows, model_width = tokens.shape
    width_loc = w_out.shape[0]
    hidden_loc = w_up.shape[1]
    clips = max(1, local_rows // CLIP_LEN)
    sharers = max(1, CLIP_LEN // local_rows)
    halves = 2 if width_loc % (2 * LANES) == 0 and replica_count % 2 == 0 and sharers == 1 else 1
    width_half, hidden_half = width_loc // halves, hidden_loc // halves
    core = lax.axis_index("dp") % halves
    part_ids = [core, 1 - core][:halves]

    def half_of(whole, axis):
        if halves == 1:
            return whole
        size = whole.shape[axis] // halves
        return lax.dynamic_slice_in_dim(whole, core * size, size, axis)

    def all_halves(half, axis):
        gathered = lax.all_gather(half, "tensor", axis=axis, tiled=True)
        if halves == 1:
            return [gathered]
        swap = [(pos, pos ^ 1) for pos in range(replica_count)]
        return [gathered, lax.ppermute(gathered, "dp", swap)]

    def in_order(parts, axis):
        if halves == 1:
            return parts[0]
        return jnp.where(core == 0, jnp.concatenate(parts, axis), jnp.concatenate(parts[::-1], axis))

    def vector_part(vector, part_id, width):
        return lax.dynamic_index_in_dim(vector.reshape(tensor_count, halves, width), part_id, 1, False)

    low = jnp.bfloat16
    row_ids = tensor_pos * local_rows + jnp.arange(local_rows, dtype=jnp.int32)
    live_rows = (row_ids // CLIP_LEN < clip_counts[0]).astype(jnp.float32)
    grad_rows = (cotangent.astype(jnp.float32) * live_rows[:, None]).astype(low)

    qkv_half = half_of(w_qkv.astype(low).reshape(model_width, 3, width_loc), 2)
    qkv_ws = all_halves(qkv_half.reshape(model_width, 3 * width_half), 1)
    out_ws = all_halves(half_of(w_out.astype(low), 0), 0)
    up_ws = all_halves(half_of(w_up.astype(low), 1), 1)
    down_ws = all_halves(half_of(w_down.astype(low), 0), 0)

    inputs_f = tokens.astype(jnp.float32)
    normed_one, inv_one = layer_norm(inputs_f)
    ln_one = (normed_one * norm_params[0] + norm_params[1]).astype(low)

    def split_heads(rows_qkv):
        parts = jnp.moveaxis(rows_qkv.reshape(local_rows, tensor_count, 3, width_half), 2, 0)
        parts = parts.reshape(3, local_rows, tensor_count * width_half)
        return [parts[0]] + [share(part) for part in parts[1:]]

    def share(part):
        others = [
            lax.ppermute(part, "tensor", [(pos, pos ^ step) for pos in range(tensor_count)])
            for step in range(1, sharers)
        ]
        return jnp.concatenate([part] + others, axis=0)

    def unshare(grad):
        pieces = grad.reshape(sharers, local_rows, grad.shape[1])
        total = pieces[0].astype(jnp.float32)
        for step in range(1, sharers):
            back = lax.ppermute(pieces[step], "tensor", [(pos, pos ^ step) for pos in range(tensor_count)])
            total = total + back.astype(jnp.float32)
        return total.astype(low)

    joined = width_half % LANES == 0 and width_half == LANES and sharers == 1
    qkvs, contexts, log_sums = [], [], []
    for qkv_w, part_id in zip(qkv_ws, part_ids):
        bias_q = vector_part(head_bias[0], part_id, width_half)
        bias_v = vector_part(head_bias[1], part_id, width_half)
        bias = jnp.stack([bias_q, jnp.zeros_like(bias_q), bias_v], axis=1).reshape(-1)
        rows_qkv = (times(ln_one, qkv_w) + bias).astype(low)
        arrays = [rows_qkv] if joined else split_heads(rows_qkv)
        context, log_sum = attention_forward(arrays, clips)
        qkvs.append(arrays)
        contexts.append(context)
        log_sums.append(log_sum)
    attn_sum = sum(times(context, out_w) for context, out_w in zip(contexts, out_ws))
    resid_one = inputs_f + attn_sum + norm_params[2]
    normed_two, inv_two = layer_norm(resid_one)
    ln_two = (normed_two * norm_params[3] + norm_params[4]).astype(low)

    hiddens, slopes = [], []
    for up_w, part_id in zip(up_ws, part_ids):
        bias = vector_part(up_bias, part_id, hidden_half).reshape(-1)
        hidden, slope = gelu_parts(times(ln_two, up_w) + bias)
        hidden, slope = lax.optimization_barrier((hidden.astype(low), slope.astype(low)))
        hiddens.append(hidden)
        slopes.append(slope)
    ffn_sum = sum(times(hidden, down_w) for hidden, down_w in zip(hiddens, down_ws))
    block_out = (resid_one + ffn_sum + norm_params[5]).astype(low)

    def scatter(grad, axis):
        return lax.psum_scatter(grad.astype(low), "tensor", scatter_dimension=axis, tiled=True).astype(jnp.float32)

    grads_pre, up_bias_parts, down_parts, up_parts = [], [], [], []
    for hidden, slope, down_w in zip(hiddens, slopes, down_ws):
        grad_pre = (times_trans(grad_rows, down_w) * slope.astype(jnp.float32)).astype(low)
        grads_pre.append(grad_pre)
        up_bias_parts.append(jnp.sum(grad_pre.astype(jnp.float32), axis=0).reshape(tensor_count, hidden_half))
        down_parts.append(scatter(inner_rows(hidden, grad_rows), 0))
        up_parts.append(scatter(inner_rows(ln_two, grad_pre), 1))
    grad_ln_two = sum(times_trans(grad_pre, up_w) for grad_pre, up_w in zip(grads_pre, up_ws))
    grad_down = in_order(down_parts, 0)
    grad_up = in_order(up_parts, 1)
    grad_res_one = grad_rows.astype(jnp.float32) + norm_back(
        grad_ln_two * norm_params[3], normed_two, inv_two
    )
    gain_two_grad = jnp.sum(grad_ln_two * normed_two, axis=0)
    shift_two_grad = jnp.sum(grad_ln_two, axis=0)
    down_bias_grad = jnp.sum(grad_rows.astype(jnp.float32), axis=0)
    out_bias_grad = jnp.sum(grad_res_one, axis=0)
    grad_attn = grad_res_one.astype(low)

    out_parts, qkv_parts, bias_parts, grads_in = [], [], [], []
    for context, log_sum, arrays, out_w, qkv_w in zip(contexts, log_sums, qkvs, out_ws, qkv_ws):
        out_parts.append(scatter(inner_rows(context, grad_attn), 0))
        grad_context = times_trans(grad_attn, out_w).astype(low)
        grads = attention_backward(arrays, context, log_sum, grad_context, clips)
        if joined:
            grad_qkv = grads[0]
        else:
            grads = [grads[0]] + [unshare(grad) for grad in grads[1:]]
            grads = [grad.reshape(local_rows, tensor_count, 1, width_half) for grad in grads]
            grad_qkv = jnp.concatenate(grads, axis=2).reshape(local_rows, -1)
        qkv_parts.append(scatter(inner_rows(ln_one, grad_qkv), 1))
        bias_parts.append(jnp.sum(grad_qkv.astype(jnp.float32), axis=0).reshape(tensor_count, 3, width_half))
        grads_in.append(times_trans(grad_qkv, qkv_w))
    grad_out_w = in_order(out_parts, 0)
    grad_qkv_w = in_order([part.reshape(model_width, 3, width_half) for part in qkv_parts], 2)
    grad_qkv_w = grad_qkv_w.reshape(model_width, 3 * width_loc)
    grad_ln_one = sum(grads_in)

    def whole_vector(parts):
        parts = [part[:, None, :] for part in parts]
        return in_order(parts, 1).reshape(-1)

    grad_head_bias = jnp.stack([whole_vector([part[:, pos] for part in bias_parts]) for pos in (0, 2)])
    grad_up_bias = whole_vector(up_bias_parts)
    grad_input = grad_res_one + norm_back(grad_ln_one * norm_params[0], normed_one, inv_one)
    input_grad = grad_input.astype(low)
    gain_one_grad = jnp.sum(grad_ln_one * normed_one, axis=0)
    shift_one_grad = jnp.sum(grad_ln_one, axis=0)
    grad_norm = jnp.stack(
        [
            gain_one_grad,
            shift_one_grad,
            out_bias_grad,
            gain_two_grad,
            shift_two_grad,
            down_bias_grad,
        ]
    )
    sum_norm, sum_head, sum_up = lax.psum(
        (grad_norm, grad_head_bias, grad_up_bias), ("dp", "tensor")
    )
    new_vecs = []
    new_vec_moms = []
    for param_now, moment_now, grad_sum in zip(
        (norm_params, head_bias, up_bias),
        (mom_norm, mom_head_bias, mom_up_bias),
        (sum_norm, sum_head, sum_up),
    ):
        moment_new = MOMENTUM_DECAY * moment_now + grad_sum / replica_count
        new_vec_moms.append(moment_new)
        new_vecs.append(param_now - VECTOR_RATE * moment_new)
    grads_local = (grad_qkv_w, grad_out_w, grad_up, grad_down)
    errors_local = (err_qkv.reshape(model_width, 3 * width_loc), err_out[0], err_up[0], err_down[0])
    factors_local = (basis_qkv[0], basis_out[0], basis_up[0], basis_down[0])
    merged = [grad_now + error_now for grad_now, error_now in zip(grads_local, errors_local)]
    lefts = [
        dot_on(0, 1, factor, matrix, PRECISE) for matrix, factor in zip(merged, factors_local)
    ]
    orthos = orthonormal(psum_joined(lefts, "dp"))
    rights = [times(ortho_left, matrix, PRECISE) for matrix, ortho_left in zip(merged, orthos)]
    right_means = [right_sum / replica_count for right_sum in psum_joined(rights, "dp")]
    approxs = [
        inner_rows(ortho_left, right_mean, PRECISE)
        for ortho_left, right_mean in zip(orthos, right_means)
    ]
    new_errs = [matrix - approx for matrix, approx in zip(merged, approxs)]
    natural_shapes = (
        (model_width, 3, width_loc),
        (width_loc, model_width),
        (model_width, hidden_loc),
        (hidden_loc, model_width),
    )
    weights = (w_qkv, w_out, w_up, w_down)
    moments = (mom_qkv, mom_out, mom_up, mom_down)
    new_weights = []
    new_moments = []
    new_errors = []
    for weight, moment, approx, new_err, shape_now in zip(
        weights, moments, approxs, new_errs, natural_shapes
    ):
        moment_new = MOMENTUM_DECAY * moment + approx.reshape(shape_now)
        new_moments.append(moment_new)
        new_weights.append(weight - STEP_RATE * moment_new)
        new_errors.append(new_err.reshape((1,) + shape_now))
    return (
        block_out,
        input_grad,
        new_vecs[0],
        new_vecs[1],
        new_vecs[2],
        new_weights[0],
        new_weights[1],
        new_weights[2],
        new_weights[3],
        new_vec_moms[0],
        new_vec_moms[1],
        new_vec_moms[2],
        new_moments[0],
        new_moments[1],
        new_moments[2],
        new_moments[3],
        new_errors[0],
        new_errors[1],
        new_errors[2],
        new_errors[3],
        orthos[0].T[None],
        orthos[1].T[None],
        orthos[2].T[None],
        orthos[3].T[None],
        right_means[0].T[None],
        right_means[1].T[None],
        right_means[2].T[None],
        right_means[3].T[None],
    )


def solution(mesh):
    in_specs = (
        P(("dp", "tensor"), None),
        P(("dp", "tensor"), None),
        P("dp"),
        P(),
        P(),
        P(),
        P(None, None, "tensor"),
        P("tensor", None),
        P(None, "tensor"),
        P("tensor", None),
        P(),
        P(),
        P(),
        P(None, None, "tensor"),
        P("tensor", None),
        P(None, "tensor"),
        P("tensor", None),
        P("dp", None, None, "tensor"),
        P("dp", "tensor", None),
        P("dp", None, "tensor"),
        P("dp", "tensor", None),
        P("tensor", None, None),
        P("tensor", None, None),
        P("tensor", None, None),
        P("tensor", None, None),
    )
    out_specs = (
        P(("dp", "tensor"), None),
        P(("dp", "tensor"), None),
        P(),
        P(),
        P(),
        P(None, None, "tensor"),
        P("tensor", None),
        P(None, "tensor"),
        P("tensor", None),
        P(),
        P(),
        P(),
        P(None, None, "tensor"),
        P("tensor", None),
        P(None, "tensor"),
        P("tensor", None),
        P("dp", None, None, "tensor"),
        P("dp", "tensor", None),
        P("dp", None, "tensor"),
        P("dp", "tensor", None),
        P("tensor", None, None),
        P("tensor", None, None),
        P("tensor", None, None),
        P("tensor", None, None),
        P("tensor", None, None),
        P("tensor", None, None),
        P("tensor", None, None),
        P("tensor", None, None),
    )
    return jax.shard_map(shards, mesh=mesh, in_specs=in_specs, out_specs=out_specs, check_vma=False)
```

```python
import functools

import jax
import jax.numpy as jnp
from jax import lax
from jax.experimental import pallas as pl
from jax.experimental.pallas import tpu as pltpu
from jax.sharding import PartitionSpec as P


HEAD_DIM = 64
CLIP_LEN = 1024
LANES = 128
DP, TENSOR = "dp", "tensor"

PRECISE = lax.Precision.HIGHEST
NORM_EPS = 1e-06
STEP_RATE = 0.001
VECTOR_RATE = 0.015
MOMENTUM_DECAY = 0.9


def layer_norm(values):
    centre = values - jnp.mean(values, axis=-1, keepdims=True)
    spread = jnp.mean(centre * centre, axis=-1, keepdims=True)
    inv_std = lax.rsqrt(spread + NORM_EPS)
    return (centre * inv_std, inv_std)


def norm_back(grad_norm, normed, inv_std):
    mean_grad = jnp.mean(grad_norm, axis=-1, keepdims=True)
    mean_cross = jnp.mean(grad_norm * normed, axis=-1, keepdims=True)
    return inv_std * (grad_norm - mean_grad - normed * mean_cross)


def dot_on(left_dim, right_dim, left_mat, right_mat, precision=None):
    return lax.dot_general(
        left_mat,
        right_mat,
        (((left_dim,), (right_dim,)), ((), ())),
        precision=precision,
        preferred_element_type=jnp.float32,
    )


inner_rows = functools.partial(dot_on, 0, 0)
times_trans = functools.partial(dot_on, 1, 1)
times = functools.partial(dot_on, 1, 0)


def gelu_parts(pre_act):
    size = jnp.abs(pre_act) * (0.5**0.5)
    bell = jnp.exp(-size * size)
    inv = 1.0 / (1.0 + 0.3275911 * size)
    series = 1.061405429 * inv - 1.453152027
    series = series * inv + 1.421413741
    series = series * inv - 0.284496736
    series = series * inv + 0.254829592
    tail = 0.5 * series * inv * bell
    cdf = jnp.where(pre_act >= 0, 1.0 - tail, tail)
    return (pre_act * cdf, cdf + pre_act * bell * 0.3989422804014327)


def head_masks(rows):
    lane = lax.broadcasted_iota(jnp.int32, (rows, LANES), 1)
    return [lane // HEAD_DIM == pos for pos in range(LANES // HEAD_DIM)]


def only(mask, values):
    return jnp.where(mask, values, jnp.zeros_like(values))


def forward_body(scale, tile, q_ref, k_ref, v_ref, ctx_ref, lse_ref, k_heads, v_heads):
    masks = head_masks(k_ref.shape[0])
    for pos, mask in enumerate(masks):
        k_heads[pos] = only(mask, k_ref[...])
        v_heads[pos, :, :LANES] = only(mask, v_ref[...])
        v_heads[pos, :, LANES:] = mask.astype(jnp.bfloat16)
    tile_masks = head_masks(tile)

    def step(pos, carry):
        rows = pl.ds(pl.multiple_of(pos * tile, tile), tile)
        q_tile = q_ref[rows, :] * scale
        total = jnp.zeros((tile, 2 * LANES), jnp.float32)
        tops = []
        for head in range(len(masks)):
            scores = times_trans(q_tile, k_heads[head])
            top = jnp.max(scores, axis=1, keepdims=True)
            weights = jnp.exp(scores - top).astype(jnp.bfloat16)
            total = total + times(weights, v_heads[head])
            tops.append(top)
        sums = total[:, LANES:]
        ctx_ref[rows, :] = (total[:, :LANES] / sums).astype(jnp.bfloat16)
        lse_ref[rows, :] = jnp.where(tile_masks[0], tops[0], tops[1]) + jnp.log(sums)
        return carry

    lax.fori_loop(0, q_ref.shape[0] // tile, step, 0, unroll=True)


def backward_body(
    scale, tile, q_ref, k_ref, v_ref, ctx_ref, lse_ref, do_ref, dq_ref, dk_ref, dv_ref, k_heads, v_heads, dk_sum, dv_sum
):
    masks = head_masks(k_ref.shape[0])
    for pos, mask in enumerate(masks):
        k_heads[pos] = only(mask, k_ref[...])
        v_heads[pos] = only(mask, v_ref[...])
    tile_masks = head_masks(tile)
    dk_sum[...] = jnp.zeros_like(dk_sum)
    dv_sum[...] = jnp.zeros_like(dv_sum)

    def step(pos, carry):
        rows = pl.ds(pl.multiple_of(pos * tile, tile), tile)
        q_tile = q_ref[rows, :] * scale
        do_tile = do_ref[rows, :]
        lse = lse_ref[rows, :]
        cross = do_tile.astype(jnp.float32) * ctx_ref[rows, :].astype(jnp.float32)
        grad_q = jnp.zeros((tile, LANES), jnp.float32)
        for head, mask in enumerate(tile_masks):
            scores = times_trans(q_tile, k_heads[head])
            lane = head * HEAD_DIM
            probs = jnp.exp(scores - lse[:, lane : lane + 1])
            inner = jnp.sum(only(mask, cross), axis=1, keepdims=True)
            grad_p = times_trans(do_tile, v_heads[head])
            grad_s = (probs * (grad_p - inner)).astype(jnp.bfloat16)
            grad_q = grad_q + times(grad_s, k_heads[head])
            dk_sum[...] += inner_rows(grad_s, only(mask, q_tile))
            dv_sum[...] += inner_rows(probs.astype(jnp.bfloat16), only(mask, do_tile))
        dq_ref[rows, :] = (grad_q * scale).astype(jnp.bfloat16)
        return carry

    lax.fori_loop(0, q_ref.shape[0] // tile, step, 0, unroll=True)
    dk_ref[...] = dk_sum[...].astype(jnp.bfloat16)
    dv_ref[...] = dv_sum[...].astype(jnp.bfloat16)


def joined_forward(scale, tile, qkv_ref, *refs):
    parts = [qkv_ref.at[:, pos * LANES : (pos + 1) * LANES] for pos in range(3)]
    forward_body(scale, tile, *parts, *refs)


def joined_backward(scale, tile, qkv_ref, ctx_ref, lse_ref, do_ref, grad_ref, *scratch):
    parts = [qkv_ref.at[:, pos * LANES : (pos + 1) * LANES] for pos in range(3)]
    grads = [grad_ref.at[:, pos * LANES : (pos + 1) * LANES] for pos in range(3)]
    backward_body(scale, tile, *parts, ctx_ref, lse_ref, do_ref, *grads, *scratch)


def block_of(rows, width):
    return pl.BlockSpec((rows, width), lambda clip, block: (clip, block))


def attention_forward(arrays, clips, tile=256):
    joined = len(arrays) == 1
    q_rows, k_rows = arrays[0].shape[0] // clips, arrays[-1].shape[0] // clips
    blocks = arrays[0].shape[1] // (LANES * (3 if joined else 1))
    work = clips * blocks * 2 * q_rows * k_rows
    in_specs = [block_of(q_rows, 3 * LANES)] if joined else [block_of(q_rows, LANES), block_of(k_rows, LANES), block_of(k_rows, LANES)]
    return pl.pallas_call(
        functools.partial(joined_forward if joined else forward_body, HEAD_DIM**-0.5, min(tile, q_rows)),
        grid=(clips, blocks),
        in_specs=in_specs,
        out_specs=[block_of(q_rows, LANES), block_of(q_rows, LANES)],
        out_shape=[
            jax.ShapeDtypeStruct((clips * q_rows, blocks * LANES), dtype)
            for dtype in (jnp.bfloat16, jnp.float32)
        ],
        scratch_shapes=[
            pltpu.VMEM((2, k_rows, LANES), jnp.bfloat16),
            pltpu.VMEM((2, k_rows, 2 * LANES), jnp.bfloat16),
        ],
        cost_estimate=pl.CostEstimate(
            flops=1024 * work, transcendentals=work, bytes_accessed=12 * clips * blocks * q_rows * LANES
        ),
        name="attn_fwd",
    )(*arrays)


def attention_backward(arrays, ctx, lse, grad_ctx, clips, tile=256, grad_block=0):
    joined = len(arrays) == 1
    q_rows, k_rows = arrays[0].shape[0] // clips, arrays[-1].shape[0] // clips
    blocks = ctx.shape[1] // LANES
    work = clips * blocks * 2 * q_rows * k_rows
    shifted = pl.BlockSpec((q_rows, LANES), lambda clip, block: (clip, block + grad_block))
    shared = [block_of(q_rows, LANES), block_of(q_rows, LANES), shifted]
    if joined:
        in_specs = [block_of(q_rows, 3 * LANES)] + shared
        out_specs = [block_of(q_rows, 3 * LANES)]
        out_shape = [jax.ShapeDtypeStruct(arrays[0].shape, jnp.bfloat16)]
    else:
        in_specs = [block_of(q_rows, LANES), block_of(k_rows, LANES), block_of(k_rows, LANES)] + shared
        out_specs = [block_of(q_rows, LANES), block_of(k_rows, LANES), block_of(k_rows, LANES)]
        out_shape = [jax.ShapeDtypeStruct(array.shape, jnp.bfloat16) for array in arrays]
    return pl.pallas_call(
        functools.partial(joined_backward if joined else backward_body, HEAD_DIM**-0.5, min(tile, q_rows)),
        grid=(clips, blocks),
        in_specs=in_specs,
        out_specs=out_specs,
        out_shape=out_shape,
        scratch_shapes=[
            pltpu.VMEM((2, k_rows, LANES), jnp.bfloat16),
            pltpu.VMEM((2, k_rows, LANES), jnp.bfloat16),
            pltpu.VMEM((k_rows, LANES), jnp.float32),
            pltpu.VMEM((k_rows, LANES), jnp.float32),
        ],
        cost_estimate=pl.CostEstimate(
            flops=2560 * work, transcendentals=work, bytes_accessed=20 * clips * blocks * q_rows * LANES
        ),
        name="attn_bwd",
    )(*arrays, ctx, lse, grad_ctx)


def orthonormal_rows(values):
    values, rank = list(values), values[0].shape[0]
    rows = lax.broadcasted_iota(jnp.int32, (rank, 1), 0)
    for pos in range(rank):
        for which, value in enumerate(values):
            vector = value[pos : pos + 1, :]
            vector = vector * lax.rsqrt(jnp.sum(vector * vector, axis=1, keepdims=True) + 1e-12)
            along = jnp.sum(value * vector, axis=1, keepdims=True)
            later = jnp.where(rows > pos, value - along * vector, value)
            values[which] = jnp.where(rows == pos, vector, later)
    return values


def orthonormal_body(count, *refs):
    for ref, value in zip(refs[count:], orthonormal_rows([ref[...] for ref in refs[:count]])):
        ref[...] = value


def orthonormal(lefts):
    return pl.pallas_call(
        functools.partial(orthonormal_body, len(lefts)),
        out_shape=[jax.ShapeDtypeStruct(left.shape, jnp.float32) for left in lefts],
        name="orthonormal",
    )(*lefts)


def psum_joined(parts, axis):
    joined = lax.psum(jnp.concatenate(parts, axis=1).astype(jnp.bfloat16), axis).astype(jnp.float32)
    ends = [0]
    for part in parts:
        ends.append(ends[-1] + part.shape[1])
    return [joined[:, start:end] for start, end in zip(ends, ends[1:])]


def gelu_tile(pre_act):
    size = jnp.abs(pre_act) * (0.5**0.5)
    bell = jnp.exp(-size * size)
    below = 1.0 + 0.3275911 * size
    inv = pl.reciprocal(below, approx=True)
    inv = inv * (2.0 - below * inv)
    series = 0.5 * 1.061405429 * inv - 0.5 * 1.453152027
    series = series * inv + 0.5 * 1.421413741
    series = series * inv - 0.5 * 0.284496736
    series = series * inv + 0.5 * 0.254829592
    tail = series * inv * bell
    cdf = jnp.where(pre_act >= 0, 1.0 - tail, tail)
    return (pre_act * cdf, cdf + pre_act * bell * 0.3989422804014327)


VMEM_BYTES = 60 * 2**20


def tiled(rows, width):
    return pl.BlockSpec((rows, width), lambda step: (step, 0))


def whole(*shape, at=0):
    return pl.BlockSpec(shape, lambda step: (at,) + (0,) * (len(shape) - 1), pipeline_mode=pl.Buffered(1))


SCALARS = pl.BlockSpec(memory_space=pltpu.SMEM)


def shaped(shape, dtype):
    return jax.ShapeDtypeStruct(shape, dtype)


def row_call(body, rows, tile, flops, args, specs, outs, out_specs, scratch=(), aliases=None, moved=0):
    return pl.pallas_call(
        body,
        grid=(rows // tile,),
        in_specs=specs,
        out_specs=out_specs,
        out_shape=outs,
        scratch_shapes=list(scratch),
        input_output_aliases=aliases or {},
        compiler_params=pltpu.CompilerParams(vmem_limit_bytes=VMEM_BYTES),
        cost_estimate=pl.CostEstimate(flops=flops, transcendentals=0, bytes_accessed=moved),
    )(*args)


def row_norm(values):
    centre = values - jnp.mean(values, axis=1, keepdims=True)
    inv_std = lax.rsqrt(jnp.mean(centre * centre, axis=1, keepdims=True) + NORM_EPS)
    return (centre * inv_std, inv_std)


def fill_columns(scratch, pieces):
    start = 0
    for ref in pieces:
        scratch[:, start : start + ref.shape[1]] = ref[...]
        start += ref.shape[1]


def qkv_body(x_ref, bias_ref, near_ref, far_ref, out_ref, weight):
    @pl.when(pl.program_id(0) == 0)
    def _():
        fill_columns(weight, (near_ref, far_ref))

    out_ref[...] = (times(x_ref[...], weight[...]) + bias_ref[...]).astype(jnp.bfloat16)


def norm_qkv_body(x_ref, norm_ref, bias_ref, near_ref, far_ref, normed_ref, out_ref, weight):
    normed, _ = row_norm(x_ref[...].astype(jnp.float32))
    normed_ref[...] = (normed * norm_ref[0:1, :] + norm_ref[1:2, :]).astype(jnp.bfloat16)
    qkv_body(normed_ref, bias_ref, near_ref, far_ref, out_ref, weight)


def qkv_slot(x, bias, pieces, norm_params=None, tile=512):
    rows, depth = x.shape
    width = pieces[0].shape[1]
    args, specs = [x], [tiled(tile, depth)]
    outs, out_specs = [shaped((rows, 2 * width), jnp.bfloat16)], [tiled(tile, 2 * width)]
    if norm_params is not None:
        args.append(norm_params)
        specs.append(whole(*norm_params.shape))
        outs.insert(0, shaped((rows, depth), jnp.bfloat16))
        out_specs.insert(0, tiled(tile, depth))
    return row_call(
        qkv_body if norm_params is None else norm_qkv_body,
        rows,
        tile,
        4 * rows * depth * width,
        (*args, bias, *pieces),
        specs + [whole(1, 2 * width), whole(depth, width), whole(depth, width)],
        outs,
        out_specs,
        [pltpu.VMEM((depth, 2 * width), jnp.bfloat16)],
        moved=2 * rows * (depth + 2 * width),
    )


def fill_rows(scratch, pieces):
    start = 0
    for ref in pieces:
        scratch[start : start + ref.shape[0], :] = ref[...]
        start += ref.shape[0]


def attend_out_body(count, x_ref, norm_ref, *refs):
    ctx_refs, pieces = refs[:count], refs[count : 3 * count]
    resid_ref, low_ref, weight = refs[3 * count :]

    @pl.when(pl.program_id(0) == 0)
    def _():
        fill_rows(weight, pieces)

    context = jnp.concatenate([ref[...] for ref in ctx_refs], axis=1)
    resid = x_ref[...].astype(jnp.float32) + times(context, weight[...]) + norm_ref[2:3, :]
    normed, _ = row_norm(resid)
    resid_ref[...] = resid
    low_ref[...] = (normed * norm_ref[3:4, :] + norm_ref[4:5, :]).astype(jnp.bfloat16)


def out_specs_of(pieces, width):
    return [whole(width // 2, piece.shape[1], at=2 * piece.shape[0] // width - 1) for piece in pieces]


def attend_out(tokens, norm_params, contexts, pieces, tile=512):
    rows, depth = tokens.shape
    width = contexts[0].shape[1]
    return row_call(
        functools.partial(attend_out_body, len(contexts)),
        rows,
        tile,
        2 * rows * depth * depth,
        (tokens, norm_params, *contexts, *pieces),
        [tiled(tile, depth), whole(*norm_params.shape)]
        + [tiled(tile, width) for _ in contexts]
        + out_specs_of(pieces, width),
        [shaped((rows, depth), jnp.float32), shaped((rows, depth), jnp.bfloat16)],
        [tiled(tile, depth), tiled(tile, depth)],
        [pltpu.VMEM((width * len(contexts), depth), jnp.bfloat16)],
        moved=10 * rows * depth,
    )


def live_rows_of(live_ref, dy_ref):
    dy = dy_ref[...]
    return jnp.where(live_ref[pl.program_id(0)] > 0, dy, jnp.zeros_like(dy))


def ffn_body(first, added, live_ref, x_ref, dy_ref, bias_ref, up_near, up_far, down_near, down_far, *refs):
    refs = list(refs)
    ffn_in, mid_in = (None, None) if first else (refs.pop(0), refs.pop(0))
    add_ref = refs.pop(0) if added else None
    ffn_ref, mid_ref, grad_ref, bias_grad, grad_sum = refs
    step, last = pl.program_id(0), pl.num_programs(0) - 1
    depth = x_ref.shape[1]
    fold = depth // 2
    up_sum, down_sum = grad_sum.at[:depth], grad_sum.at[depth:]

    @pl.when(step == 0)
    def _():
        grad_sum[...] = jnp.zeros_like(grad_sum)
        bias_grad[...] = jnp.zeros_like(bias_grad)

    x, dy = x_ref[...], live_rows_of(live_ref, dy_ref)
    width = down_near.shape[0]
    ffn = None if first else ffn_in[...]
    mid = None if first else mid_in[...]
    for part, (up, down) in enumerate(((up_near, down_near), (up_far, down_far))):
        cols = slice(part * width, (part + 1) * width)
        pre = times(x[:, :fold], up[:, :fold]) + times(x[:, fold:], up[:, fold:])
        hidden, slope = gelu_tile(pre + bias_ref[:, cols])
        hidden = hidden.astype(jnp.bfloat16)
        term = times(hidden, down[...])
        ffn = term if ffn is None else ffn + term
        grad_pre = (times_trans(dy, down[...]) * slope).astype(jnp.bfloat16)
        term = jnp.concatenate([times_trans(grad_pre, up[:, :fold]), times_trans(grad_pre, up[:, fold:])], axis=1)
        mid = term if mid is None else mid + term
        down_sum[cols, :] += inner_rows(hidden, dy)
        up_sum[:, cols] += inner_rows(x, grad_pre)
        bias_grad[:, cols] += jnp.sum(grad_pre.astype(jnp.float32), axis=0, keepdims=True)
    ffn_ref[...] = ffn
    mid_ref[...] = mid

    @pl.when(step == last)
    def _():
        total = grad_sum[...]
        if added:
            total = total + add_ref[...].astype(jnp.float32)
        grad_ref[...] = total.astype(jnp.bfloat16)


def ffn_slot(live, x, dy, bias, pieces, sums, add):
    rows, depth = x.shape
    half = depth // 2
    width, tile = bias.shape[1], rows // live.shape[0]
    args = [live, x, dy, bias, *pieces, *pieces]
    specs = [SCALARS, tiled(tile, depth), tiled(tile, depth), whole(1, width)]
    specs += [whole(half, depth)] * 2 + [whole(half, depth, at=1)] * 2
    aliases = {}
    if sums is not None:
        aliases = {len(args): 0, len(args) + 1: 1}
        args += list(sums)
        specs += [tiled(tile, depth)] * 2
    if add is not None:
        args.append(add)
        specs.append(whole(2 * depth, width))
    return row_call(
        functools.partial(ffn_body, sums is None, add is not None),
        rows,
        tile,
        12 * rows * depth * width,
        args,
        specs,
        [shaped((rows, depth), jnp.float32)] * 2
        + [shaped((2 * depth, width), jnp.bfloat16), shaped((1, width), jnp.float32)],
        [tiled(tile, depth)] * 2 + [whole(2 * depth, width), whole(1, width)],
        [pltpu.VMEM((2 * depth, width), jnp.float32)],
        aliases,
        20 * rows * depth,
    )


def back_norm(grad_norm, normed, inv_std):
    mean_grad = jnp.mean(grad_norm, axis=1, keepdims=True)
    mean_cross = jnp.mean(grad_norm * normed, axis=1, keepdims=True)
    return inv_std * (grad_norm - mean_grad - normed * mean_cross)


def column_sum(values):
    return jnp.sum(values, axis=0, keepdims=True)


def middle_body(count, live_ref, resid_ref, ffn_ref, mid_ref, dy_ref, norm_ref, *refs):
    ctx_refs, pieces = refs[:count], refs[count : 3 * count]
    out_ref, grad_ref, ctx_grad_ref, sums_ref = refs[3 * count : 3 * count + 4]
    weight_grads = refs[3 * count + 4 : 4 * count + 4]
    weight, weight_sum = refs[4 * count + 4 :]
    step, last = pl.program_id(0), pl.num_programs(0) - 1

    @pl.when(step == 0)
    def _():
        fill_rows(weight, pieces)
        weight_sum[...] = jnp.zeros_like(weight_sum)
        sums_ref[...] = jnp.zeros_like(sums_ref)

    resid, grad_mid = resid_ref[...], mid_ref[...]
    dy = live_rows_of(live_ref, dy_ref).astype(jnp.float32)
    out_ref[...] = (resid + ffn_ref[...] + norm_ref[5:6, :]).astype(jnp.bfloat16)
    normed, inv_std = row_norm(resid)
    grad_resid = dy + back_norm(grad_mid * norm_ref[3:4, :], normed, inv_std)
    grad_low = grad_resid.astype(jnp.bfloat16)
    grad_ref[...] = grad_low
    ctx_grad_ref[...] = times_trans(grad_low, weight[...]).astype(jnp.bfloat16)
    context = jnp.concatenate([ref[...] for ref in ctx_refs], axis=1)
    weight_sum[...] += inner_rows(context, grad_low)
    for row, values in ((2, grad_resid), (3, grad_mid * normed), (4, grad_mid), (5, dy)):
        sums_ref[row : row + 1, :] += column_sum(values)

    @pl.when(step == last)
    def _():
        start = 0
        for ref in weight_grads:
            ref[...] = weight_sum[start : start + ref.shape[0], :].astype(jnp.bfloat16)
            start += ref.shape[0]


def middle(live, resid, ffn, mid, dy, norm_params, contexts, pieces):
    rows, depth = resid.shape
    count, width = len(contexts), contexts[0].shape[1]
    tile = rows // live.shape[0]
    return row_call(
        functools.partial(middle_body, count),
        rows,
        tile,
        4 * rows * depth * depth,
        (live, resid, ffn, mid, dy, norm_params, *contexts, *pieces),
        [SCALARS]
        + [tiled(tile, depth)] * 4
        + [whole(*norm_params.shape)]
        + [tiled(tile, width) for _ in contexts]
        + out_specs_of(pieces, width),
        [shaped((rows, depth), jnp.bfloat16)] * 2
        + [shaped((rows, width * count), jnp.bfloat16), shaped((8, depth), jnp.float32)]
        + [shaped((width, depth), jnp.bfloat16)] * count,
        [tiled(tile, depth)] * 2 + [tiled(tile, width * count), whole(8, depth)] + [whole(width, depth)] * count,
        [pltpu.VMEM((width * count, depth), jnp.bfloat16), pltpu.VMEM((width * count, depth), jnp.float32)],
        None,
        26 * rows * depth,
    )


def pack_body(core_ref, up_ref, down_ref, out_ref, near_ref, far_ref):
    first = core_ref[0] == 0
    half = down_ref.shape[0] // 2
    part = out_ref.shape[0] // 2
    ups = [up_ref[:, :half].astype(jnp.bfloat16), up_ref[:, half:].astype(jnp.bfloat16)]
    downs = [down_ref[:half, :].astype(jnp.bfloat16), down_ref[half:, :].astype(jnp.bfloat16)]
    outs = [out_ref[:part, :].astype(jnp.bfloat16), out_ref[part:, :].astype(jnp.bfloat16)]
    for pos, ref in enumerate((near_ref, far_ref)):
        up = jnp.where(first, ups[pos], ups[1 - pos])
        fold = up.shape[0] // 2
        ref[:half, :half] = up[:fold, :]
        ref[:half, half:] = up[fold:, :]
        ref[half : 2 * half, :] = jnp.where(first, downs[pos], downs[1 - pos])
        ref[2 * half :, :] = jnp.where(first, outs[pos], outs[1 - pos])


def pack(core, w_up, w_down, w_out):
    shape = ((w_down.shape[0] + w_out.shape[0]) // 2 + w_up.shape[0] // 2, w_down.shape[1])
    return pl.pallas_call(
        pack_body,
        in_specs=[SCALARS] + [pl.BlockSpec(memory_space=pltpu.VMEM)] * 3,
        out_shape=[shaped(shape, jnp.bfloat16)] * 2,
        compiler_params=pltpu.CompilerParams(vmem_limit_bytes=VMEM_BYTES),
        cost_estimate=pl.CostEstimate(flops=0, transcendentals=0, bytes_accessed=6 * (w_up.size + w_down.size + w_out.size)),
        name="pack",
    )(core, w_up, w_down, w_out)


def split_low(values):
    high = values.astype(jnp.bfloat16)
    return high, (values - high.astype(jnp.float32)).astype(jnp.bfloat16)


def left_body(kind, core_ref, own_ref, one_ref, two_ref, err_ref, basis_ref, merged_ref, left_ref):
    total = own_ref[...].astype(jnp.float32) + one_ref[...].astype(jnp.float32) + two_ref[...].astype(jnp.float32)
    first = core_ref[0] == 0
    width = total.shape[1] // 2
    if kind == ROWS:
        merged_ref[...] = total + err_ref[0]
    elif kind == COLS:
        near, far = total[:, :width], total[:, width:]
        merged_ref[:, :width] = jnp.where(first, near, far) + err_ref[0, :, :width]
        merged_ref[:, width:] = jnp.where(first, far, near) + err_ref[0, :, width:]
    else:
        for col in range(3):
            parts = [total[:, half * width + col * LANES : half * width + (col + 1) * LANES] for half in range(2)]
            error = err_ref[0, :, col, :]
            for half in range(2):
                start = (2 * col + half) * LANES
                piece = jnp.where(first, parts[half], parts[1 - half])
                merged_ref[:, start : start + LANES] = piece + error[:, half * LANES : (half + 1) * LANES]
    high, rest = split_low(merged_ref[...])
    rank = left_ref.shape[0]
    by_high = jnp.transpose(times(high, basis_ref[...]))
    by_rest = jnp.transpose(times(rest, basis_ref[...]))
    left_ref[...] = by_high[:rank] + by_high[rank : 2 * rank] + by_rest[:rank]


ROWS, COLS, HEADS = 0, 1, 2


def left_factor(kind, core, grads, error, basis, start=0, tile=256):
    rows, width = error.shape[1], basis.shape[1]
    rank = basis.shape[2]
    tile = min(tile, rows // 2)
    count = rows // tile
    high, rest = split_low(basis[0])
    packed = jnp.concatenate([high, rest, jnp.zeros((width, LANES - 2 * rank), jnp.bfloat16)], axis=1)

    def grad_at(step, core_ref):
        moved = (step + core_ref[0] * (count // 2)) % count if kind == ROWS else step
        return (start // tile + moved, 0)

    trailing = error.shape[2:]
    return pl.pallas_call(
        functools.partial(left_body, kind),
        grid_spec=pltpu.PrefetchScalarGridSpec(
            num_scalar_prefetch=1,
            grid=(count,),
            in_specs=[pl.BlockSpec((tile, width), grad_at)] * 3
            + [
                pl.BlockSpec((1, tile) + trailing, lambda step, core_ref: (0, step) + (0,) * len(trailing)),
                pl.BlockSpec((width, LANES), lambda step, core_ref: (0, 0)),
            ],
            out_specs=[
                pl.BlockSpec((tile, width), lambda step, core_ref: (step, 0)),
                pl.BlockSpec((rank, tile), lambda step, core_ref: (0, step)),
            ],
        ),
        out_shape=[shaped((rows, width), jnp.float32), shaped((rank, rows), jnp.float32)],
        cost_estimate=pl.CostEstimate(flops=1024 * rows * width, transcendentals=0, bytes_accessed=14 * rows * width),
        name="left",
    )(core, *grads, error, packed)


def stack_low(values, order):
    parts = split_low(values)
    return jnp.concatenate([parts[which] for which in order], axis=0)


def ortho_body(sizes, own_ref, *refs):
    others, outs = refs[:3], refs[3:]
    total = [ref[...].astype(jnp.float32) for ref in (own_ref, *others)]
    total = (total[0] + total[1]) + (total[2] + total[3])
    values, start = [], 0
    for size in sizes:
        values.append(total[:, start : start + size])
        start += size
    values = orthonormal_rows(values)
    for pos, value in enumerate(values):
        outs[2 * pos][...] = value
        outs[2 * pos + 1][...] = stack_low(value, (0, 1, 0))


def ortho_sum(sizes, parts):
    rank = parts[0].shape[0]
    outs = []
    for size in sizes:
        outs += [shaped((rank, size), jnp.float32), shaped((3 * rank, size), jnp.bfloat16)]
    return pl.pallas_call(functools.partial(ortho_body, sizes), out_shape=outs, name="ortho")(*parts)


def mean_body(replicas, own_ref, one_ref, two_ref, three_ref, mean_ref, low_ref):
    total = [ref[...].astype(jnp.float32) for ref in (own_ref, one_ref, two_ref, three_ref)]
    mean = ((total[0] + total[1]) + (total[2] + total[3])) / replicas
    mean_ref[...] = mean
    low_ref[...] = stack_low(mean, (0, 0, 1))


def mean_sum(replicas, parts):
    rank, size = parts[0].shape
    return pl.pallas_call(
        functools.partial(mean_body, replicas),
        out_shape=[shaped((rank, size), jnp.float32), shaped((3 * rank, size), jnp.bfloat16)],
        name="mean",
    )(*parts)


def right_body(ortho_ref, merged_ref, right_ref):
    @pl.when(pl.program_id(0) == 0)
    def _():
        right_ref[...] = jnp.zeros_like(right_ref)

    high, rest = split_low(merged_ref[...])
    rank = right_ref.shape[0]
    by_high, by_rest = times(ortho_ref[...], high), times(ortho_ref[...], rest)
    right_ref[...] += by_high[:rank] + by_high[rank : 2 * rank] + by_rest[:rank]


def right_factor(ortho_low, merged, tile=256):
    rows, width = merged.shape
    rank = ortho_low.shape[0] // 3
    return pl.pallas_call(
        right_body,
        grid=(rows // tile,),
        in_specs=[pl.BlockSpec((3 * rank, tile), lambda step: (0, step)), tiled(tile, width)],
        out_specs=pl.BlockSpec((rank, width), lambda step: (0, 0)),
        out_shape=shaped((rank, width), jnp.float32),
        cost_estimate=pl.CostEstimate(flops=1024 * rows * width, transcendentals=0, bytes_accessed=4 * rows * width),
        name="right",
    )(ortho_low, merged)


def update_body(ortho_ref, mean_ref, merged_ref, moment_ref, weight_ref, error_out, moment_out, weight_out):
    approx = inner_rows(ortho_ref[...], mean_ref[...])
    merged = merged_ref[...]
    if len(moment_ref.shape) == 2:
        error_out[0] = merged - approx
        moment = MOMENTUM_DECAY * moment_ref[...] + approx
        moment_out[...] = moment
        weight_out[...] = weight_ref[...] - STEP_RATE * moment
        return
    width = moment_ref.shape[2]
    for col in range(moment_ref.shape[1]):
        cols = slice(col * width, (col + 1) * width)
        error_out[0, :, col, :] = merged[:, cols] - approx[:, cols]
        moment = MOMENTUM_DECAY * moment_ref[:, col, :] + approx[:, cols]
        moment_out[:, col, :] = moment
        weight_out[:, col, :] = weight_ref[:, col, :] - STEP_RATE * moment


def update(ortho_low, mean_low, merged, moment, weight, tile=256):
    rows, width = merged.shape
    stacked = ortho_low.shape[0]
    trailing = moment.shape[1:]
    natural = pl.BlockSpec((tile,) + trailing, lambda step: (step,) + (0,) * len(trailing))
    error = pl.BlockSpec((1, tile) + trailing, lambda step: (0, step) + (0,) * len(trailing))
    return pl.pallas_call(
        update_body,
        grid=(rows // tile,),
        in_specs=[
            pl.BlockSpec((stacked, tile), lambda step: (0, step)),
            pl.BlockSpec((stacked, width), lambda step: (0, 0)),
            tiled(tile, width),
            natural,
            natural,
        ],
        out_specs=[error, natural, natural],
        out_shape=[shaped((1, rows) + trailing, jnp.float32)] + [shaped(moment.shape, jnp.float32)] * 2,
        cost_estimate=pl.CostEstimate(flops=512 * rows * width, transcendentals=0, bytes_accessed=24 * rows * width),
        name="update",
    )(ortho_low, mean_low, merged, moment, weight)


def first_norm_body(count, x_ref, grad_ref, norm_ref, *refs):
    grad_qkvs, pieces = refs[:count], refs[count : 3 * count]
    out_ref, sums_ref, bias_ref, weight = refs[3 * count :]

    @pl.when(pl.program_id(0) == 0)
    def _():
        fill_columns(weight, pieces)
        sums_ref[...] = jnp.zeros_like(sums_ref)
        bias_ref[...] = jnp.zeros_like(bias_ref)

    grad_qkv = jnp.concatenate([ref[...] for ref in grad_qkvs], axis=1)
    grad_in = times_trans(grad_qkv, weight[...])
    normed, inv_std = row_norm(x_ref[...].astype(jnp.float32))
    back = back_norm(grad_in * norm_ref[0:1, :], normed, inv_std)
    out_ref[...] = (grad_ref[...].astype(jnp.float32) + back).astype(jnp.bfloat16)
    sums_ref[0:1, :] += column_sum(grad_in * normed)
    sums_ref[1:2, :] += column_sum(grad_in)
    bias_ref[...] += column_sum(grad_qkv.astype(jnp.float32))


def first_norm(tokens, grad, norm_params, grad_qkvs, pieces, tile=256):
    rows, depth = tokens.shape
    count, width = len(grad_qkvs), grad_qkvs[0].shape[1]
    return row_call(
        functools.partial(first_norm_body, count),
        rows,
        tile,
        2 * rows * depth * width * count,
        (tokens, grad, norm_params, *grad_qkvs, *pieces),
        [tiled(tile, depth)] * 2
        + [whole(*norm_params.shape)]
        + [tiled(tile, width) for _ in grad_qkvs]
        + [whole(*piece.shape) for piece in pieces],
        [shaped((rows, depth), jnp.bfloat16), shaped((8, depth), jnp.float32), shaped((1, width * count), jnp.float32)],
        [tiled(tile, depth), whole(8, depth), whole(1, width * count)],
        [pltpu.VMEM((depth, width * count), jnp.bfloat16)],
        None,
        6 * rows * depth + 2 * rows * width * count,
    )


def shards_any(
    tokens,
    cotangent,
    clip_counts,
    norm_params,
    head_bias,
    up_bias,
    w_qkv,
    w_out,
    w_up,
    w_down,
    mom_norm,
    mom_head_bias,
    mom_up_bias,
    mom_qkv,
    mom_out,
    mom_up,
    mom_down,
    err_qkv,
    err_out,
    err_up,
    err_down,
    basis_qkv,
    basis_out,
    basis_up,
    basis_down,
):
    tensor_count = lax.axis_size(TENSOR)
    tensor_pos = lax.axis_index(TENSOR)
    replica_count = lax.axis_size(DP)
    local_rows, model_width = tokens.shape
    width_loc = w_out.shape[0]
    hidden_loc = w_up.shape[1]
    clips = max(1, local_rows // CLIP_LEN)
    sharers = max(1, CLIP_LEN // local_rows)
    halves = 2 if width_loc % (2 * LANES) == 0 and replica_count % 2 == 0 and sharers == 1 else 1
    width_half, hidden_half = width_loc // halves, hidden_loc // halves
    core = lax.axis_index(DP) % halves
    part_ids = [core, 1 - core][:halves]

    def half_of(whole, axis):
        if halves == 1:
            return whole
        size = whole.shape[axis] // halves
        return lax.dynamic_slice_in_dim(whole, core * size, size, axis)

    def all_halves(half, axis):
        gathered = lax.all_gather(half, TENSOR, axis=axis, tiled=True)
        if halves == 1:
            return [gathered]
        swap = [(pos, pos ^ 1) for pos in range(replica_count)]
        return [gathered, lax.ppermute(gathered, DP, swap)]

    def in_order(parts, axis):
        if halves == 1:
            return parts[0]
        return jnp.where(core == 0, jnp.concatenate(parts, axis), jnp.concatenate(parts[::-1], axis))

    def vector_part(vector, part_id, width):
        return lax.dynamic_index_in_dim(vector.reshape(tensor_count, halves, width), part_id, 1, False)

    low = jnp.bfloat16
    row_ids = tensor_pos * local_rows + jnp.arange(local_rows, dtype=jnp.int32)
    live_rows = (row_ids // CLIP_LEN < clip_counts[0]).astype(jnp.float32)
    grad_rows = (cotangent.astype(jnp.float32) * live_rows[:, None]).astype(low)

    qkv_half = half_of(w_qkv.astype(low).reshape(model_width, 3, width_loc), 2)
    qkv_ws = all_halves(qkv_half.reshape(model_width, 3 * width_half), 1)
    out_ws = all_halves(half_of(w_out.astype(low), 0), 0)
    up_ws = all_halves(half_of(w_up.astype(low), 1), 1)
    down_ws = all_halves(half_of(w_down.astype(low), 0), 0)

    inputs_f = tokens.astype(jnp.float32)
    normed_one, inv_one = layer_norm(inputs_f)
    ln_one = (normed_one * norm_params[0] + norm_params[1]).astype(low)

    def split_heads(rows_qkv):
        parts = jnp.moveaxis(rows_qkv.reshape(local_rows, tensor_count, 3, width_half), 2, 0)
        parts = parts.reshape(3, local_rows, tensor_count * width_half)
        return [parts[0]] + [share(part) for part in parts[1:]]

    def share(part):
        others = [
            lax.ppermute(part, TENSOR, [(pos, pos ^ step) for pos in range(tensor_count)])
            for step in range(1, sharers)
        ]
        return jnp.concatenate([part] + others, axis=0)

    def unshare(grad):
        pieces = grad.reshape(sharers, local_rows, grad.shape[1])
        total = pieces[0].astype(jnp.float32)
        for step in range(1, sharers):
            back = lax.ppermute(pieces[step], TENSOR, [(pos, pos ^ step) for pos in range(tensor_count)])
            total = total + back.astype(jnp.float32)
        return total.astype(low)

    joined = width_half % LANES == 0 and width_half == LANES and sharers == 1
    qkvs, contexts, log_sums = [], [], []
    for qkv_w, part_id in zip(qkv_ws, part_ids):
        bias_q = vector_part(head_bias[0], part_id, width_half)
        bias_v = vector_part(head_bias[1], part_id, width_half)
        bias = jnp.stack([bias_q, jnp.zeros_like(bias_q), bias_v], axis=1).reshape(-1)
        rows_qkv = (times(ln_one, qkv_w) + bias).astype(low)
        arrays = [rows_qkv] if joined else split_heads(rows_qkv)
        context, log_sum = attention_forward(arrays, clips)
        qkvs.append(arrays)
        contexts.append(context)
        log_sums.append(log_sum)
    attn_sum = sum(times(context, out_w) for context, out_w in zip(contexts, out_ws))
    resid_one = inputs_f + attn_sum + norm_params[2]
    normed_two, inv_two = layer_norm(resid_one)
    ln_two = (normed_two * norm_params[3] + norm_params[4]).astype(low)

    hiddens, slopes = [], []
    for up_w, part_id in zip(up_ws, part_ids):
        bias = vector_part(up_bias, part_id, hidden_half).reshape(-1)
        hidden, slope = gelu_parts(times(ln_two, up_w) + bias)
        hidden, slope = lax.optimization_barrier((hidden.astype(low), slope.astype(low)))
        hiddens.append(hidden)
        slopes.append(slope)
    ffn_sum = sum(times(hidden, down_w) for hidden, down_w in zip(hiddens, down_ws))
    block_out = (resid_one + ffn_sum + norm_params[5]).astype(low)

    def scatter(grad, axis):
        return lax.psum_scatter(grad.astype(low), TENSOR, scatter_dimension=axis, tiled=True).astype(jnp.float32)

    grads_pre, up_bias_parts, down_parts, up_parts = [], [], [], []
    for hidden, slope, down_w in zip(hiddens, slopes, down_ws):
        grad_pre = (times_trans(grad_rows, down_w) * slope.astype(jnp.float32)).astype(low)
        grads_pre.append(grad_pre)
        up_bias_parts.append(jnp.sum(grad_pre.astype(jnp.float32), axis=0).reshape(tensor_count, hidden_half))
        down_parts.append(scatter(inner_rows(hidden, grad_rows), 0))
        up_parts.append(scatter(inner_rows(ln_two, grad_pre), 1))
    grad_ln_two = sum(times_trans(grad_pre, up_w) for grad_pre, up_w in zip(grads_pre, up_ws))
    grad_down = in_order(down_parts, 0)
    grad_up = in_order(up_parts, 1)
    grad_res_one = grad_rows.astype(jnp.float32) + norm_back(
        grad_ln_two * norm_params[3], normed_two, inv_two
    )
    gain_two_grad = jnp.sum(grad_ln_two * normed_two, axis=0)
    shift_two_grad = jnp.sum(grad_ln_two, axis=0)
    down_bias_grad = jnp.sum(grad_rows.astype(jnp.float32), axis=0)
    out_bias_grad = jnp.sum(grad_res_one, axis=0)
    grad_attn = grad_res_one.astype(low)

    out_parts, qkv_parts, bias_parts, grads_in = [], [], [], []
    for context, log_sum, arrays, out_w, qkv_w in zip(contexts, log_sums, qkvs, out_ws, qkv_ws):
        out_parts.append(scatter(inner_rows(context, grad_attn), 0))
        grad_context = times_trans(grad_attn, out_w).astype(low)
        grads = attention_backward(arrays, context, log_sum, grad_context, clips)
        if joined:
            grad_qkv = grads[0]
        else:
            grads = [grads[0]] + [unshare(grad) for grad in grads[1:]]
            grads = [grad.reshape(local_rows, tensor_count, 1, width_half) for grad in grads]
            grad_qkv = jnp.concatenate(grads, axis=2).reshape(local_rows, -1)
        qkv_parts.append(scatter(inner_rows(ln_one, grad_qkv), 1))
        bias_parts.append(jnp.sum(grad_qkv.astype(jnp.float32), axis=0).reshape(tensor_count, 3, width_half))
        grads_in.append(times_trans(grad_qkv, qkv_w))
    grad_out_w = in_order(out_parts, 0)
    grad_qkv_w = in_order([part.reshape(model_width, 3, width_half) for part in qkv_parts], 2)
    grad_qkv_w = grad_qkv_w.reshape(model_width, 3 * width_loc)
    grad_ln_one = sum(grads_in)

    def whole_vector(parts):
        parts = [part[:, None, :] for part in parts]
        return in_order(parts, 1).reshape(-1)

    grad_head_bias = jnp.stack([whole_vector([part[:, pos] for part in bias_parts]) for pos in (0, 2)])
    grad_up_bias = whole_vector(up_bias_parts)
    grad_input = grad_res_one + norm_back(grad_ln_one * norm_params[0], normed_one, inv_one)
    input_grad = grad_input.astype(low)
    gain_one_grad = jnp.sum(grad_ln_one * normed_one, axis=0)
    shift_one_grad = jnp.sum(grad_ln_one, axis=0)
    grad_norm = jnp.stack(
        [
            gain_one_grad,
            shift_one_grad,
            out_bias_grad,
            gain_two_grad,
            shift_two_grad,
            down_bias_grad,
        ]
    )
    sum_norm, sum_head, sum_up = lax.psum(
        (grad_norm, grad_head_bias, grad_up_bias), (DP, TENSOR)
    )
    new_vecs = []
    new_vec_moms = []
    for param_now, moment_now, grad_sum in zip(
        (norm_params, head_bias, up_bias),
        (mom_norm, mom_head_bias, mom_up_bias),
        (sum_norm, sum_head, sum_up),
    ):
        moment_new = MOMENTUM_DECAY * moment_now + grad_sum / replica_count
        new_vec_moms.append(moment_new)
        new_vecs.append(param_now - VECTOR_RATE * moment_new)
    grads_local = (grad_qkv_w, grad_out_w, grad_up, grad_down)
    errors_local = (err_qkv.reshape(model_width, 3 * width_loc), err_out[0], err_up[0], err_down[0])
    factors_local = (basis_qkv[0], basis_out[0], basis_up[0], basis_down[0])
    merged = [grad_now + error_now for grad_now, error_now in zip(grads_local, errors_local)]
    lefts = [
        dot_on(0, 1, factor, matrix, PRECISE) for matrix, factor in zip(merged, factors_local)
    ]
    orthos = orthonormal(psum_joined(lefts, DP))
    rights = [times(ortho_left, matrix, PRECISE) for matrix, ortho_left in zip(merged, orthos)]
    right_means = [right_sum / replica_count for right_sum in psum_joined(rights, DP)]
    approxs = [
        inner_rows(ortho_left, right_mean, PRECISE)
        for ortho_left, right_mean in zip(orthos, right_means)
    ]
    new_errs = [matrix - approx for matrix, approx in zip(merged, approxs)]
    natural_shapes = (
        (model_width, 3, width_loc),
        (width_loc, model_width),
        (model_width, hidden_loc),
        (hidden_loc, model_width),
    )
    weights = (w_qkv, w_out, w_up, w_down)
    moments = (mom_qkv, mom_out, mom_up, mom_down)
    new_weights = []
    new_moments = []
    new_errors = []
    for weight, moment, approx, new_err, shape_now in zip(
        weights, moments, approxs, new_errs, natural_shapes
    ):
        moment_new = MOMENTUM_DECAY * moment + approx.reshape(shape_now)
        new_moments.append(moment_new)
        new_weights.append(weight - STEP_RATE * moment_new)
        new_errors.append(new_err.reshape((1,) + shape_now))
    return (
        block_out,
        input_grad,
        new_vecs[0],
        new_vecs[1],
        new_vecs[2],
        new_weights[0],
        new_weights[1],
        new_weights[2],
        new_weights[3],
        new_vec_moms[0],
        new_vec_moms[1],
        new_vec_moms[2],
        new_moments[0],
        new_moments[1],
        new_moments[2],
        new_moments[3],
        new_errors[0],
        new_errors[1],
        new_errors[2],
        new_errors[3],
        orthos[0].T[None],
        orthos[1].T[None],
        orthos[2].T[None],
        orthos[3].T[None],
        right_means[0].T[None],
        right_means[1].T[None],
        right_means[2].T[None],
        right_means[3].T[None],
    )


def shards_four(
    tokens,
    cotangent,
    clip_counts,
    norm_params,
    head_bias,
    up_bias,
    w_qkv,
    w_out,
    w_up,
    w_down,
    mom_norm,
    mom_head_bias,
    mom_up_bias,
    mom_qkv,
    mom_out,
    mom_up,
    mom_down,
    err_qkv,
    err_out,
    err_up,
    err_down,
    basis_qkv,
    basis_out,
    basis_up,
    basis_down,
):
    pos, core = lax.axis_index(TENSOR), lax.axis_index(DP) % 2
    count, replica_count = lax.axis_size(TENSOR), lax.axis_size(DP)
    local_rows, model_width = tokens.shape
    width_loc = w_out.shape[0]
    width_half = width_loc // 2
    clips = local_rows // CLIP_LEN
    low, full = jnp.bfloat16, jnp.float32

    def steps(first, second):
        return [
            (dp * count + place, dp * count + (place ^ (second if dp % 2 else first)))
            for dp in range(replica_count)
            for place in range(count)
        ]

    def by_a(array):
        return lax.ppermute(array, (DP, TENSOR), steps(1, 2))

    def by_b(array):
        return lax.ppermute(array, (DP, TENSOR), steps(2, 1))

    def over_dp(array, step):
        return lax.ppermute(array, DP, [(dp, dp ^ step) for dp in range(replica_count)])

    def over_tensor(array, step):
        return lax.ppermute(array, TENSOR, [(place, place ^ step) for place in range(count)])

    def gather(pieces):
        near, far = pieces
        one, two = by_a(near), by_b(near)
        three = by_b(one)
        pairs = [(near, far)]
        for ours, theirs in ((one, two), (two, one), (three, three)):
            pairs.append((ours, over_dp(theirs, 1)))
        return pairs

    def swap_if(flag, array, axis):
        return jnp.where(flag, jnp.flip(array, axis), array)

    def flip_places(array):
        return swap_if(pos // 2 == 1, swap_if(pos % 2 == 1, array, 1), 0)

    def to_slots(vector):
        array = flip_places(vector.reshape(2, 2, 2, -1))
        array = jnp.where(core == 1, jnp.swapaxes(array, 0, 1), array)
        return swap_if(core == 1, array, 2).reshape(count, 1, -1)

    def from_slots(parts):
        array = swap_if(core == 1, parts.reshape(2, 2, 2, -1), 2)
        array = jnp.where(core == 1, jnp.swapaxes(array, 0, 1), array)
        return flip_places(array).reshape(-1)

    def qkv_piece(which):
        parts = [
            lax.dynamic_slice(w_qkv, (0, col, which * width_half), (model_width, 1, width_half))
            for col in range(3)
        ]
        return jnp.concatenate([part.reshape(model_width, width_half) for part in parts], axis=1).astype(low)

    qkv_ws = gather([qkv_piece(core), qkv_piece(1 - core)])
    core_word = core.astype(jnp.int32).reshape(1)
    rest_ws = gather(pack(core_word, w_up, w_down, w_out))
    rest_pieces = [part for pair in rest_ws for part in pair]
    qkv_pieces = [part for pair in qkv_ws for part in pair]

    live_tile = CLIP_LEN // 2
    tile_ids = pos * local_rows + jnp.arange(local_rows // live_tile, dtype=jnp.int32) * live_tile
    live = (tile_ids // CLIP_LEN < clip_counts[0]).astype(jnp.int32)

    biases = [to_slots(bias) for bias in (head_bias[0], head_bias[1], up_bias)]
    halves_q, halves_v = [bias.reshape(count, 2, width_half) for bias in biases[:2]]
    qkv_bias = jnp.stack([halves_q, jnp.zeros_like(halves_q), halves_v], axis=2).reshape(count, 1, -1)
    qkvs, contexts, log_sums = [], [], []
    for slot in range(count):
        if slot == 0:
            ln_one, qkv = qkv_slot(tokens, qkv_bias[slot], qkv_ws[slot], norm_params)
        else:
            (qkv,) = qkv_slot(ln_one, qkv_bias[slot], qkv_ws[slot])
        context, log_sum = attention_forward([qkv], clips)
        qkvs.append(qkv)
        contexts.append(context)
        log_sums.append(log_sum)
    resid, ln_two = attend_out(tokens, norm_params, contexts, rest_pieces)

    sums, ffn_grads, up_bias_grads = None, [None] * 4, [None] * 4
    for slot in (0, 3, 1, 2):
        add = by_a(ffn_grads[3]) if slot == 2 else None
        ffn, mid, ffn_grads[slot], up_bias_grads[slot] = ffn_slot(
            live, ln_two, cotangent, biases[2][slot], rest_ws[slot], sums, add
        )
        sums = (ffn, mid)
    block_out, grad_attn, grad_context, middle_sums, *out_grads = middle(
        live, resid, *sums, cotangent, norm_params, contexts, rest_pieces
    )

    def arrived(grads):
        return [grads[0], by_a(grads[1]), by_b(grads[2])]

    out_grads[2] = (out_grads[2].astype(full) + by_a(out_grads[3]).astype(full)).astype(low)
    grad_qkvs, qkv_grads = [None] * 4, [None] * 4
    for slot in (3, 1, 2, 0):
        (grad_qkvs[slot],) = attention_backward(
            [qkvs[slot]], contexts[slot], log_sums[slot], grad_context, clips, grad_block=2 * slot
        )
        grad_w = inner_rows(ln_one, grad_qkvs[slot])
        if slot == 2:
            grad_w = grad_w + by_a(qkv_grads[3]).astype(full)
        qkv_grads[slot] = grad_w.astype(low)
    input_grad, first_sums, qkv_bias_sums = first_norm(tokens, grad_attn, norm_params, grad_qkvs, qkv_pieces)

    qkv_bias_sums = qkv_bias_sums.reshape(count, 2, 3, width_half)
    grad_head_bias = jnp.stack([from_slots(qkv_bias_sums[:, :, which].reshape(count, -1)) for which in (0, 2)])
    grad_up_bias = from_slots(jnp.concatenate(up_bias_grads, axis=0))
    grad_norm = jnp.concatenate([first_sums[:2], middle_sums[2:6]], axis=0)
    vector_grads = jnp.concatenate([grad_norm.reshape(-1), grad_head_bias.reshape(-1), grad_up_bias]).reshape(-1, LANES)

    def sum_dp(array):
        pair = array.astype(full) + over_dp(array, 1).astype(full)
        pair = pair.astype(array.dtype)
        return [pair] + [over_dp(pair, step) for step in range(2, replica_count, 2)]

    def tree(values):
        while len(values) > 1:
            values = [left + right for left, right in zip(values[::2], values[1::2])]
        return values[0]

    vector_sums = tree(sum_dp(vector_grads))
    vector_sums = tree([vector_sums] + [over_tensor(vector_sums, step) for step in range(1, count)]).reshape(-1)
    ends = [6 * model_width, 8 * model_width]
    sum_norm, sum_head, sum_up = jnp.split(vector_sums, ends)
    sum_norm, sum_head = sum_norm.reshape(6, model_width), sum_head.reshape(2, model_width)

    def compress(entries):
        merged, lefts = [], []
        for kind, grads, error, basis, start in entries:
            matrix, left = left_factor(kind, core_word, grads, error, basis, start)
            merged.append(matrix)
            lefts.append(left.astype(low))
        sizes = [left.shape[1] for left in lefts]
        orthos = ortho_sum(sizes, sum_dp(jnp.concatenate(lefts, axis=1)))
        ortho_lows = orthos[1::2]
        rights = [right_factor(*pair).astype(low) for pair in zip(ortho_lows, merged)]
        mean, mean_low = mean_sum(replica_count, sum_dp(jnp.concatenate(rights, axis=1)))
        cuts, results = 0, []
        for matrix, ortho, ortho_low, right in zip(merged, orthos[::2], ortho_lows, rights):
            ends = cuts + right.shape[1]
            results.append((ortho_low, mean_low[:, cuts:ends], matrix, ortho, mean[:, cuts:ends]))
            cuts = ends
        return results

    ffn_arrived = arrived(ffn_grads)
    up_parts, down_parts, out_parts = compress(
        [
            (COLS, ffn_arrived, err_up, basis_up, 0),
            (ROWS, ffn_arrived, err_down, basis_down, model_width),
            (ROWS, arrived(out_grads), err_out, basis_out, 0),
        ],
    )
    (qkv_parts,) = compress([(HEADS, arrived(qkv_grads), err_qkv, basis_qkv, 0)])
    new_vecs = []
    new_vec_moms = []
    for param_now, moment_now, grad_sum in zip(
        (norm_params, head_bias, up_bias),
        (mom_norm, mom_head_bias, mom_up_bias),
        (sum_norm, sum_head, sum_up),
    ):
        moment_new = MOMENTUM_DECAY * moment_now + grad_sum / replica_count
        new_vec_moms.append(moment_new)
        new_vecs.append(param_now - VECTOR_RATE * moment_new)
    parts = (qkv_parts, out_parts, up_parts, down_parts)
    orthos, right_means = [part[3] for part in parts], [part[4] for part in parts]
    new_errors, new_moments, new_weights = [], [], []
    for pos, (part, moment, weight) in enumerate(
        zip(parts, (mom_qkv, mom_out, mom_up, mom_down), (w_qkv, w_out, w_up, w_down))
    ):
        error_new, moment_new, weight_new = update(*part[:3], moment, weight)
        new_errors.append(error_new)
        new_moments.append(moment_new)
        new_weights.append(weight_new)
    return (
        block_out,
        input_grad,
        new_vecs[0],
        new_vecs[1],
        new_vecs[2],
        new_weights[0],
        new_weights[1],
        new_weights[2],
        new_weights[3],
        new_vec_moms[0],
        new_vec_moms[1],
        new_vec_moms[2],
        new_moments[0],
        new_moments[1],
        new_moments[2],
        new_moments[3],
        new_errors[0],
        new_errors[1],
        new_errors[2],
        new_errors[3],
        orthos[0].T[None],
        orthos[1].T[None],
        orthos[2].T[None],
        orthos[3].T[None],
        right_means[0].T[None],
        right_means[1].T[None],
        right_means[2].T[None],
        right_means[3].T[None],
    )


def shards(*arrays):
    tokens, w_out, w_up = arrays[0], arrays[7], arrays[8]
    aligned = w_out.shape[0] == 2 * LANES and w_up.shape[1] % (4 * LANES) == 0
    if is_square() and aligned and tokens.shape[0] % CLIP_LEN == 0:
        return shards_four(*arrays)
    return shards_any(*arrays)


def is_square():
    return lax.axis_size(TENSOR) == 4 and lax.axis_size(DP) == 8


def solution(mesh):
    in_specs = (
        P((DP, TENSOR), None),
        P((DP, TENSOR), None),
        P(DP),
        P(),
        P(),
        P(),
        P(None, None, TENSOR),
        P(TENSOR, None),
        P(None, TENSOR),
        P(TENSOR, None),
        P(),
        P(),
        P(),
        P(None, None, TENSOR),
        P(TENSOR, None),
        P(None, TENSOR),
        P(TENSOR, None),
        P(DP, None, None, TENSOR),
        P(DP, TENSOR, None),
        P(DP, None, TENSOR),
        P(DP, TENSOR, None),
        P(TENSOR, None, None),
        P(TENSOR, None, None),
        P(TENSOR, None, None),
        P(TENSOR, None, None),
    )
    out_specs = (
        P((DP, TENSOR), None),
        P((DP, TENSOR), None),
        P(),
        P(),
        P(),
        P(None, None, TENSOR),
        P(TENSOR, None),
        P(None, TENSOR),
        P(TENSOR, None),
        P(),
        P(),
        P(),
        P(None, None, TENSOR),
        P(TENSOR, None),
        P(None, TENSOR),
        P(TENSOR, None),
        P(DP, None, None, TENSOR),
        P(DP, TENSOR, None),
        P(DP, None, TENSOR),
        P(DP, TENSOR, None),
        P(TENSOR, None, None),
        P(TENSOR, None, None),
        P(TENSOR, None, None),
        P(TENSOR, None, None),
        P(TENSOR, None, None),
        P(TENSOR, None, None),
        P(TENSOR, None, None),
        P(TENSOR, None, None),
    )
    return jax.shard_map(shards, mesh=mesh, in_specs=in_specs, out_specs=out_specs, check_vma=False)
```
